256 devices in a mesh: dp: 8 (over z_lo, core), seq: 16 (over x, y), mp: 2 (over z_hi).
Axes of the slice: x: 4, y: 4, z: 8 (z_hi: 2, z_lo: 4; z = z_hi * 4 + z_lo), core: 2. Of those that a mesh axis runs over, the one named last changes fastest.
Arguments:
- features: bfloat16 [8, 8192, 1408], P('dp', ('seq', 'mp')), may hold values from -6 to 6
- conv_weight: bfloat16 [5, 1408, 1536], P(None, ('seq', 'mp')), may hold values from -0.0625 to 0.0625
- norm_gain: float32 [1536], replicated, may hold values from 0.25 to 1.75
- query_weight: bfloat16 [1536, 1024], replicated, may hold values from -0.15625 to 0.15625
- keyval_weight: bfloat16 [1536, 320], replicated, may hold values from -0.15625 to 0.15625
- head_scale: float32 [8], replicated, may hold values from 0.5 to 24
- output_weight: bfloat16 [1536, 1536], replicated, may hold values from -0.15625 to 0.15625
- pair_weight: bfloat16 [1536, 256], replicated, may hold values from -0.625 to 0.625
- pair_input: bfloat16 [8, 256, 256, 128], P('dp', ('seq', 'mp')), may hold values from -6 to 6
- flip_weight: bfloat16 [128, 128], replicated, may hold values from -0.5 to 0.5
- pair_cotangent: bfloat16 [8, 256, 256, 128], P('dp', ('seq', 'mp')), may hold values from -0.0234375 to 0.0234375
Outputs:
- block_out: bfloat16 [8, 4096, 1536], P('dp', ('seq', 'mp'))
- pair_out: bfloat16 [8, 256, 256, 128], P('dp', ('seq', 'mp'))
- grad_flip: float32 [128, 128], replicated
The draws below stay inside these ranges and needn't reach their ends.
All inputs are finite; a program needn't handle non-finite values.
Results may differ from the reference program's by a relative error of at most 0.011.
Values may be sent and summed in bfloat16 or wider, within the bound.
A program may use at most 192 MiB of HBM per device.

```python
import math
import jax
import jax.numpy as jnp
from jax import lax

CIN = 1408
D = 1536
HEADS = 8
DK = 128
DV = 192
PC = 128
KW = 5
PAIR_POOL = 16
BATCH = 8
POS = 4096
PR = 256


def block_scale(stream_key, shape, shards, low, largest):
    def one(position, shards_of):
        draws = jax.random.uniform(jax.random.fold_in(jax.random.fold_in(stream_key, 6), position), (shards_of,), jnp.float32, low / len(shards), largest / len(shards))
        return jnp.repeat(jnp.exp(draws), shape[position] // shards_of).reshape((-1,) + (1,) * (len(shape) - position - 1))

    loudness = one(*shards[0])
    for cut in shards[1:]:
        loudness = loudness * one(*cut)
    return loudness


def scatter_about(key, shape, scale, most, shards=(), held_as=jnp.bfloat16):
    level = block_scale(key, shape, shards, -0.22, 0.18) if shards else 1.0
    array = jax.random.normal(key, shape, jnp.float32) * scale * level
    return jnp.minimum(jnp.maximum(array, -most), most).astype(held_as)


def setup_inputs(seed: int = 0) -> dict:
    splits = jax.random.split(jax.random.key(seed), 12)
    return {
        "features": scatter_about(splits[0], (BATCH, 2 * POS, CIN), 1.0, 6.0, ((0, 8), (1, 32))),
        "conv_weight": scatter_about(splits[1], (KW, CIN, D), (KW * CIN) ** -0.5, 0.0625, ((1, 32),)),
        "norm_gain": jnp.clip(1.0 + 0.15 * jax.random.normal(splits[2], (D,), jnp.float32), 0.25, 1.75),
        "query_weight": scatter_about(splits[3], (D, HEADS * DK), D ** -0.5, 0.15625),
        "keyval_weight": scatter_about(splits[4], (D, DK + DV), D ** -0.5, 0.15625),
        "head_scale": jnp.clip(jnp.exp(jax.random.uniform(splits[5], (HEADS,), jnp.float32, math.log(0.5), math.log(24.0))), 0.5, 24.0),
        "output_weight": scatter_about(splits[6], (HEADS * DV, D), (HEADS * DV) ** -0.5, 0.15625),
        "pair_weight": scatter_about(splits[7], (D, 2 * PC), (D // 16) ** -0.5, 0.625),
        "pair_input": scatter_about(splits[8], (BATCH, PR, PR, PC), 1.0, 6.0, ((0, 8), (1, 32))),
        "flip_weight": scatter_about(splits[9], (PC, PC), PC ** -0.5, 0.5),
        "pair_cotangent": scatter_about(splits[10], (BATCH, PR, PR, PC), (1.0 / PR), 0.0234375, ((0, 8), (1, 32))),
    }


norm_eps = 1e-06
logit_cap = 50.0

def root_norm(values_in):
    return values_in * lax.rsqrt(lax.optimization_barrier(jnp.mean(values_in * values_in, axis=-1, keepdims=True)) + norm_eps)

def prepare(raw):
    return jax.nn.gelu(root_norm(raw.astype(jnp.float32)), approximate=False).astype(jnp.bfloat16)

def one_window(features, pair_input, pair_cotangent, conv_weight, norm_gain, query_weight, keyval_weight, head_scale, output_weight, pair_weight, flip_weight):
    fine_len = features.shape[0]
    margin = KW // 2
    prepared = prepare(features)
    padded = jnp.pad(prepared, ((margin, margin), (0, 0)))
    conv_sum = jnp.zeros((fine_len, D), jnp.float32)
    for lag_index in range(KW):
        conv_sum = conv_sum + jnp.dot(padded[lag_index:lag_index + fine_len], conv_weight[lag_index], preferred_element_type=jnp.float32)
    skipped = jnp.pad(features.astype(jnp.float32), ((0, 0), (0, D - CIN)))
    encoded = lax.optimization_barrier(jnp.max((conv_sum + skipped).reshape(fine_len // 2, 2, D), axis=1)).astype(jnp.bfloat16)
    widened = encoded.astype(jnp.float32)
    normed = (root_norm(widened) * norm_gain).astype(jnp.bfloat16)
    scale_row = jnp.repeat(head_scale, DK) / math.sqrt(DK)
    queries = (jnp.dot(normed, query_weight, preferred_element_type=jnp.float32) * scale_row).astype(jnp.bfloat16)
    keyvals = jnp.dot(normed, keyval_weight, preferred_element_type=jnp.float32).astype(jnp.bfloat16)
    key_rows = keyvals[:, :DK]
    value_rows = keyvals[:, DK:]
    block_len = math.gcd(POS, 512)
    query_blocks = queries.reshape(POS // block_len, block_len * HEADS, DK)

    def attend(query_block):
        scores = jnp.dot(query_block, key_rows.T, preferred_element_type=jnp.float32)
        weights = jnp.exp(logit_cap * jnp.tanh(scores / logit_cap))
        totals = lax.optimization_barrier(jnp.sum(weights, axis=-1, keepdims=True))
        mixed = jnp.dot(weights.astype(jnp.bfloat16), value_rows, preferred_element_type=jnp.float32) / totals
        return mixed.astype(jnp.bfloat16)
    heads_out = lax.map(attend, query_blocks).reshape(POS, HEADS * DV)
    block_out = (widened + jnp.dot(heads_out, output_weight, preferred_element_type=jnp.float32)).astype(jnp.bfloat16)
    pooled = lax.optimization_barrier(jnp.mean(widened.reshape(POS // PAIR_POOL, PAIR_POOL, D), axis=1)).astype(jnp.bfloat16)
    pair_feats = jnp.dot(pooled, pair_weight, preferred_element_type=jnp.float32).astype(jnp.bfloat16)
    pair_q = pair_feats[:, :PC].astype(jnp.float32)
    pair_k = pair_feats[:, PC:].astype(jnp.float32)
    summed = (pair_input.astype(jnp.float32) + pair_q[:, None, :] * pair_k[None, :, :]).astype(jnp.bfloat16)
    flipped = jnp.swapaxes(summed, 0, 1).astype(jnp.float32)
    turned = jnp.einsum('abc,cd->abd', flipped, flip_weight.astype(jnp.float32), precision=lax.Precision.HIGHEST)
    pair_out = (summed.astype(jnp.float32) + turned).astype(jnp.bfloat16)
    grad_part = jnp.einsum('abc,abd->cd', flipped, pair_cotangent.astype(jnp.float32), precision=lax.Precision.HIGHEST)
    return (block_out, pair_out, grad_part)

def reference(features, conv_weight, norm_gain, query_weight, keyval_weight, head_scale, output_weight, pair_weight, pair_input, flip_weight, pair_cotangent):

    def per_window(packed):
        return one_window(packed[0], packed[1], packed[2], conv_weight, norm_gain, query_weight, keyval_weight, head_scale, output_weight, pair_weight, flip_weight)
    block_out, pair_out, grad_parts = lax.map(per_window, (features, pair_input, pair_cotangent))
    return (block_out, pair_out, lax.optimization_barrier(jnp.sum(grad_parts, axis=0)))
```

```python
import functools
import math

import jax
import jax.numpy as jnp
import numpy as np
from jax import lax
from jax.experimental import pallas as pl
from jax.experimental.pallas import tpu as pltpu
from jax.sharding import PartitionSpec as P

MESH = pl.DeviceIdType.MESH
PAIR_POOL = 16
SIDE = 4
CORES = 2
Z_LO = 4
norm_eps = 1e-06
logit_cap = 50.0


def root_norm(values_in):
    return values_in * lax.rsqrt(jnp.mean(values_in * values_in, axis=-1, keepdims=True) + norm_eps)


def prepare(raw):
    return jax.nn.gelu(root_norm(raw.astype(jnp.float32)), approximate=False).astype(jnp.bfloat16)


def rcopy(src, dst, ssem, rsem, dev):
    return pltpu.make_async_remote_copy(
        src_ref=src, dst_ref=dst, send_sem=ssem, recv_sem=rsem, device_id=dev, device_id_type=MESH
    )


class Gather:
    def __init__(self, buf, own_src, rows, cut, zsend, zrecv, ssem, rsem, lsem, mirror=False):
        self.mirror = mirror
        self.buf, self.own_src, self.rows, self.cut = buf, own_src, rows, cut
        self.zsend, self.zrecv, self.ssem, self.rsem, self.lsem = zsend, zrecv, ssem, rsem, lsem
        self.dp, self.seq, self.mp = (lax.axis_index(a) for a in ("dp", "seq", "mp"))
        self.x, self.y = self.seq // SIDE, self.seq % SIDE
        self.count = 0
        self.sent = []
        self.pending_local = []

    def z_partner(self):
        if not self.mirror:
            return {"mp": 1 - self.mp}
        core, z = self.dp % CORES, self.dp // CORES
        return {"dp": (Z_LO - 1 - z) * CORES + core, "mp": 1 - self.mp}

    def peers(self):
        out = [self.z_partner()]
        for q in (0, 1):
            for d in (1, -1):
                out.append({"seq": self.bid(q, d, 0)})
        return out

    def bid(self, q, da, db):
        first, second = (self.x, self.y) if q == 0 else (self.y, self.x)
        a, b = (first + da + SIDE) % SIDE, (second + db + SIDE) % SIDE
        return a * SIDE + b if q == 0 else b * SIDE + a

    def z_of(self, zsel):
        return self.mp if zsel == 0 else 1 - self.mp

    def view(self, q, zsel, da, db, half):
        ref = self.buf.at[q, self.z_of(zsel), self.bid(q, da, db)]
        if half == 0:
            return ref.at[pl.ds(0, self.cut)]
        if half == 1:
            return ref.at[pl.ds(self.cut, self.rows - self.cut)]
        return ref

    def sem(self, q, zsel, da, db, half):
        return self.rsem.at[q, self.z_of(zsel), self.bid(q, da, db), 1 if half == 1 else 0]

    def send(self, q, zsel, da, db, half, to, src=None):
        view = self.view(q, zsel, da, db, half)
        copy = rcopy(view if src is None else src, view, self.ssem.at[self.count],
                     self.sem(q, zsel, da, db, half), {"seq": self.bid(q, *to)})
        self.count += 1
        copy.start()
        self.sent.append(copy)

    def recv(self, q, zsel, da, db, half=None):
        view = self.view(q, zsel, da, db, half)
        rcopy(view, view, self.ssem.at[0], self.sem(q, zsel, da, db, half), {"seq": self.bid(q, 1, 0)}).wait_recv()

    def start_z(self):
        for q in (0, 1):
            copy = rcopy(self.own_src(q), self.view(q, 0, 0, 0, None), self.zsend.at[q], self.zrecv.at[q], self.z_partner())
            copy.start()
            self.sent.append(copy)
            local = pltpu.make_async_copy(self.own_src(q), self.view(q, 0, 0, 0, None), self.lsem.at[q])
            local.start()
            self.pending_local.append(local)

    def stage(self, q, zsel, n):
        if n == 0:
            src = self.own_src(q) if zsel == 0 else None
            if zsel == 1:
                view = self.view(q, 1, 0, 0, None)
                rcopy(view, view, self.zsend.at[q], self.zrecv.at[q], self.z_partner()).wait_recv()
            for to in ((1, 0), (-1, 0), (0, 1), (0, -1)):
                self.send(q, zsel, 0, 0, None, to, src)
        elif n in (1, 2):
            d = -1 if n == 1 else 1
            self.recv(q, zsel, d, 0)
            self.send(q, zsel, d, 0, 0 if n == 1 else 1, (-d, 0))
            for to in ((0, 1), (0, -1)):
                self.send(q, zsel, d, 0, None, to)
        elif n == 4:
            self.recv(q, zsel, 2, 0, 0)
            self.recv(q, zsel, 2, 0, 1)
            for to in ((0, 1), (0, -1)):
                self.send(q, zsel, 2, 0, None, to)
        elif n in (3, 5, 6, 7):
            da = {3: 0, 5: -1, 6: 1, 7: 2}[n]
            for d, half in ((-1, 0), (1, 1)):
                self.recv(q, zsel, da, d)
                self.send(q, zsel, da, d, half, (0, -d))
        else:
            for da in (0, -1, 1, 2):
                for half in (0, 1):
                    self.recv(q, zsel, da, 2, half)

    def drain(self):
        for copy in self.sent:
            copy.wait_send()


ORDER = [(0, 0), (0, 1), (0, 2), (0, 3), (1, 0), (0, 4), (0, 5), (0, 6), (1, 1), (1, 2), (0, 7), (1, 3), (1, 4), (1, 5), (1, 6), (1, 7)]
GATHER_SENDS = 80


def gather_sems():
    dma = pltpu.SemaphoreType.DMA
    return [dma((2,)), dma((2,)), dma((GATHER_SENDS,)), dma((2, 2, SIDE * SIDE, 2)), dma((2,))]


def greet(peers):
    barrier = pltpu.get_barrier_semaphore()
    for peer in peers:
        pl.semaphore_signal(barrier, inc=1, device_id=peer, device_id_type=MESH)
    pl.semaphore_wait(barrier, len(peers))


def conv_kernel(
    w_ref, prep_ref, edge_ref, skip_ref, chan_ref, enc_ref,
    F, X, P2, S2, H, acc, stage, zs, zr, ss, rs, ls, xs, xr,
):
    dp, seq, mp = (lax.axis_index(a) for a in ("dp", "seq", "mp"))
    core = dp % CORES
    other = dp - core + (1 - core)
    rows, cut = w_ref.shape[1], 112
    taps, depth = 5, rows // 5
    width = w_ref.shape[2]
    g = Gather(F, lambda q: w_ref.at[CORES * core + q], rows, cut, zs, zr, ss, rs, ls, mirror=True)
    place = seq * 2 + mp
    last_place = SIDE * SIDE * 2 - 1
    after, before = (place + 1) % (last_place + 1), (place + last_place) % (last_place + 1)

    def at(p, d):
        return {"dp": d, "seq": p // 2, "mp": p % 2}

    partner = {"dp": other}
    greet(g.peers() + [partner, at(after, dp), at(after, other), at(before, dp), at(before, other)])

    g.start_z()
    extra = []
    n = 0
    for w, d in ((0, dp), (1, other)):
        extra.append(rcopy(edge_ref.at[1], H.at[w, 0], xs.at[n], xr.at[n], at(after, d)))
        extra.append(rcopy(edge_ref.at[0], H.at[w, 1], xs.at[n + 1], xr.at[n + 1], at(before, d)))
        n += 2
    extra.append(rcopy(prep_ref, P2, xs.at[4], xr.at[4], partner))
    extra.append(rcopy(skip_ref.at[pl.ds(CORES * (1 - core), 2)], S2, xs.at[5], xr.at[5], partner))
    for copy in extra:
        copy.start()
    for q in (0, 1):
        g.stage(q, 0, 0)

    def spread(w, n):
        zabs, lanes = n // 3, pl.ds((n % 3) * 256, 256)
        chan = chan_ref[:, n * 256 : (n + 1) * 256]
        cin = prep_ref.shape[2]
        pick = (lax.broadcasted_iota(jnp.int32, (cin, 256), 0) == chan).astype(jnp.float32).astype(jnp.bfloat16)
        src = prep_ref if w == 0 else P2
        height = src.shape[1]
        dot = functools.partial(jnp.dot, preferred_element_type=jnp.float32)
        even, odd = dot(src[0], pick), dot(src[1], pick)
        prev, nxt = dot(H[w, 0], pick), dot(H[w, 1], pick)
        prev = jnp.where(place == 0, 0.0, prev)
        nxt = jnp.where(place == last_place, 0.0, nxt)
        row = lax.broadcasted_iota(jnp.int32, (height, 256), 0)
        for m, (arr, halo, shift) in enumerate((
            (even, prev[14:15], 1), (odd, prev[15:16], 1), (even, None, 0), (odd, None, 0),
            (even, nxt[0:1], -1), (odd, nxt[1:2], -1),
        )):
            if shift == 1:
                arr = jnp.where(row == 0, halo, pltpu.roll(arr, 1, 0))
            elif shift == -1:
                arr = jnp.where(row == height - 1, halo, pltpu.roll(arr, height - 1, 0))
            X[w, zabs, m, :, lanes] = arr.astype(jnp.bfloat16)

    def do_spread(k):
        w, n = divmod(k, 6)
        if k == 0:
            for copy in extra:
                copy.wait_recv()
        spread(w, n)

    todo = list(range(12))
    for i, (zsel, st) in enumerate(ORDER[1:]):
        if i >= 1 and todo:
            do_spread(todo.pop(0))
        for q in (0, 1):
            g.stage(q, zsel, st)
    while todo:
        do_spread(todo.pop(0))

    for local in g.pending_local:
        local.wait()

    def conv(zsel):
        za = g.z_of(zsel)
        for q in (0, 1):
            def tap(k, carry):
                lhs = X[:, za, pl.ds(k, 2)].reshape(acc.shape[1], -1)
                rhs = F[q, za, :, pl.ds(pl.multiple_of(k * depth, 16), depth), :].reshape(-1, width)
                acc[q] += jnp.dot(lhs, rhs, preferred_element_type=jnp.float32)
                return carry
            lax.fori_loop(0, taps, tap, 0)

    acc[...] = jnp.zeros_like(acc)
    for q in (0, 1):
        g.stage(q, 0, 8)
    conv(0)
    for q in (0, 1):
        g.stage(q, 1, 8)
    conv(1)
    half = acc.shape[1] // 2
    coarse = half // 2
    finals = []
    for q in (0, 1):
        total = acc[q, half:] + S2[q].astype(jnp.float32)
        stage[q] = jnp.maximum(total[:coarse], total[coarse:]).astype(jnp.bfloat16)
        copy = rcopy(stage.at[q], enc_ref.at[CORES * core + q], xs.at[6 + q], xr.at[6 + q], partner)
        copy.start()
        finals.append(copy)
    for q in (0, 1):
        total = acc[q, :half] + skip_ref[CORES * core + q].astype(jnp.float32)
        enc_ref[CORES * core + q] = jnp.maximum(total[:coarse], total[coarse:]).astype(jnp.bfloat16)
    for q in (0, 1):
        view = enc_ref.at[CORES * (1 - core) + q]
        rcopy(stage.at[q], view, xs.at[6 + q], xr.at[6 + q], partner).wait_recv()
    g.drain()
    for copy in extra + finals:
        copy.wait_send()


def encode(w4, prep, edge, skip, chan):
    vm = pl.BlockSpec(memory_space=pltpu.VMEM)
    dma = pltpu.SemaphoreType.DMA
    quarters, rows, width = w4.shape
    coarse = prep.shape[1]
    kdepth = SIDE * SIDE * rows // 5
    return pl.pallas_call(
        conv_kernel,
        out_shape=jax.ShapeDtypeStruct((quarters, coarse, width), jnp.bfloat16),
        in_specs=[vm] * 5,
        out_specs=vm,
        scratch_shapes=[
            pltpu.VMEM((2, 2, SIDE * SIDE, rows, width), jnp.bfloat16),
            pltpu.VMEM((2, 2, 6, coarse, kdepth), jnp.bfloat16),
            pltpu.VMEM(prep.shape, jnp.bfloat16),
            pltpu.VMEM((2, 2 * coarse, width), jnp.bfloat16),
            pltpu.VMEM((2, 2, 16, prep.shape[2]), jnp.bfloat16),
            pltpu.VMEM((2, 4 * coarse, width), jnp.float32),
            pltpu.VMEM((2, coarse, width), jnp.bfloat16),
        ] + gather_sems() + [dma((8,)), dma((8,))],
        compiler_params=pltpu.CompilerParams(collective_id=0, has_side_effects=True, vmem_limit_bytes=60 << 20),
        name="encode",
    )(w4, prep, edge, skip, chan)


def share_kernel(src_ref, out_ref, zs, zr, ss, rs, ls):
    rows = src_ref.shape[1]
    g = Gather(out_ref, lambda q: src_ref.at[q], rows, rows // 2, zs, zr, ss, rs, ls)
    greet(g.peers())
    g.start_z()
    for zsel, st in ORDER + [(0, 8), (1, 8)]:
        for q in (0, 1):
            g.stage(q, zsel, st)
    for local in g.pending_local:
        local.wait()
    g.drain()


def share(src):
    vm = pl.BlockSpec(memory_space=pltpu.VMEM)
    return pl.pallas_call(
        share_kernel,
        out_shape=jax.ShapeDtypeStruct((2, 2, SIDE * SIDE) + src.shape[1:], src.dtype),
        in_specs=[vm],
        out_specs=vm,
        scratch_shapes=gather_sems(),
        compiler_params=pltpu.CompilerParams(collective_id=1, has_side_effects=True, vmem_limit_bytes=32 << 20),
        name="share",
    )(src)


def total_kernel(g_ref, out_ref, R1, R2, fin, s1, r1, s2, r2, s3, r3):
    dp, seq, mp = (lax.axis_index(a) for a in ("dp", "seq", "mp"))
    n1, n2 = SIDE * SIDE, Z_LO * CORES * 2
    rows = g_ref.shape[0] // n1
    plane = [{"seq": (seq + d) % n1} for d in range(1, n1)]
    mine = dp * 2 + mp
    column = []
    for d in range(1, n2):
        t = (mine + d) % n2
        column.append({"dp": t // 2, "mp": t % 2})
    greet(plane + column)
    sent = []
    for d, dev in enumerate(plane):
        c = rcopy(g_ref.at[pl.ds(pl.multiple_of(dev["seq"] * rows, rows), rows)], R1.at[seq], s1.at[d], r1.at[seq], dev)
        c.start()
        sent.append(c)
    own = g_ref[pl.ds(pl.multiple_of(seq * rows, rows), rows)]
    R1[seq] = own
    for d, dev in enumerate(plane):
        view = R1.at[dev["seq"]]
        rcopy(view, view, s1.at[d], r1.at[dev["seq"]], dev).wait_recv()
    fin[0] = jnp.sum(R1[...], axis=0)
    for d, dev in enumerate(column):
        c = rcopy(fin.at[0], R2.at[mine], s2.at[d], r2.at[mine], dev)
        c.start()
        sent.append(c)
    R2[mine] = fin[0]
    for d, dev in enumerate(column):
        t = dev["dp"] * 2 + dev["mp"]
        rcopy(R2.at[t], R2.at[t], s2.at[d], r2.at[t], dev).wait_recv()
    fin[1] = jnp.sum(R2[...], axis=0)
    piece = pl.ds(pl.multiple_of(seq * rows, rows), rows)
    for d, dev in enumerate(plane):
        c = rcopy(fin.at[1], out_ref.at[piece], s3.at[d], r3.at[seq], dev)
        c.start()
        sent.append(c)
    out_ref[piece] = fin[1]
    for d, dev in enumerate(plane):
        view = out_ref.at[pl.ds(pl.multiple_of(dev["seq"] * rows, rows), rows)]
        rcopy(view, view, s3.at[d], r3.at[dev["seq"]], dev).wait_recv()
    for c in sent:
        c.wait_send()


def total(term):
    vm = pl.BlockSpec(memory_space=pltpu.VMEM)
    dma = pltpu.SemaphoreType.DMA
    rows = term.shape[0] // (SIDE * SIDE)
    n = SIDE * SIDE
    block = (n, rows, term.shape[1])
    return pl.pallas_call(
        total_kernel,
        out_shape=jax.ShapeDtypeStruct(term.shape, term.dtype),
        in_specs=[vm],
        out_specs=vm,
        scratch_shapes=[pltpu.VMEM(block, jnp.float32), pltpu.VMEM(block, jnp.float32), pltpu.VMEM((2,) + block[1:], jnp.float32)]
        + [dma((n,))] * 6,
        compiler_params=pltpu.CompilerParams(collective_id=2, has_side_effects=True, vmem_limit_bytes=16 << 20),
        name="total",
    )(term)


def per_device(
    features, conv_weight, norm_gain, query_weight, keyval_weight, head_scale, output_weight, pair_weight,
    pair_input, flip_weight, pair_cotangent,
):
    fine_rows, in_channels = features.shape[1:]
    coarse = fine_rows // 2
    model_dim = output_weight.shape[1]
    head_count = head_scale.shape[0]
    key_dim = query_weight.shape[1] // head_count
    value_dim = keyval_weight.shape[1] - key_dim
    pair_dim = flip_weight.shape[0]
    taps, per_shard = conv_weight.shape[:2]
    padded = 48
    quarter = model_dim // 4

    w4 = jnp.pad(conv_weight, ((0, 0), (0, padded - per_shard), (0, 0)))
    w4 = w4.reshape(taps * padded, 4, quarter).transpose(1, 0, 2)
    prepared = prepare(features[0])
    edge = jnp.stack([prepared[:16], prepared[fine_rows - 16 :]])
    prep = prepared.reshape(coarse, 2, in_channels).transpose(1, 0, 2)
    skip = jnp.pad(features[0], ((0, 0), (0, model_dim - in_channels)))
    skip = skip.reshape(coarse, 2, 4, quarter).transpose(2, 1, 0, 3).reshape(4, fine_rows, quarter)
    lane = np.arange(2 * SIDE * SIDE * padded)
    zh, sq, ch = lane // (SIDE * SIDE * padded), (lane // padded) % (SIDE * SIDE), lane % padded
    chan = np.where(ch < per_shard, per_shard * (2 * sq + zh) + ch, -1).astype(np.int32)[None]
    enc4 = encode(w4, prep, edge, skip, jnp.asarray(chan))
    encoded = enc4.transpose(1, 0, 2).reshape(coarse, model_dim)

    turned_in = lax.all_to_all(pair_input, ("seq", "mp"), split_axis=2, concat_axis=1, tiled=True)[0]

    widened = encoded.astype(jnp.float32)
    normed = (root_norm(widened) * norm_gain).astype(jnp.bfloat16)
    keyvals = jnp.dot(normed, keyval_weight, preferred_element_type=jnp.float32).astype(jnp.bfloat16)
    pooled = jnp.mean(widened.reshape(coarse // PAIR_POOL, PAIR_POOL, model_dim), axis=1).astype(jnp.bfloat16)
    feats = jnp.dot(pooled, pair_weight, preferred_element_type=jnp.float32).astype(jnp.bfloat16)
    pair_rows = feats.shape[0]
    spare = jnp.pad(feats.reshape(-1, 64), ((0, coarse - feats.size // 64), (0, 0)))
    block = jnp.concatenate([keyvals, spare], axis=1).reshape(2, coarse // 2, -1)
    shared = share(block)
    scale_row = jnp.repeat(head_scale, key_dim) / math.sqrt(key_dim)
    queries = (jnp.dot(normed, query_weight, preferred_element_type=jnp.float32) * scale_row).astype(jnp.bfloat16)

    feats_all = shared[0, :, :, : feats.size // 64, key_dim + value_dim :]
    feats_all = feats_all.transpose(1, 0, 2, 3).reshape(-1, 2 * pair_dim).astype(jnp.float32)
    pair_q, pair_k = feats[:, :pair_dim].astype(jnp.float32), feats[:, pair_dim:].astype(jnp.float32)
    q_all, k_all = feats_all[:, :pair_dim], feats_all[:, pair_dim:]
    summed = (pair_input[0].astype(jnp.float32) + pair_q[:, None, :] * k_all[None]).astype(jnp.bfloat16)
    flipped = (turned_in.astype(jnp.float32) + q_all[:, None, :] * pair_k[None]).astype(jnp.bfloat16)
    turned = jnp.einsum("bac,cd->abd", flipped, flip_weight, preferred_element_type=jnp.float32)
    pair_out = (summed.astype(jnp.float32) + turned).astype(jnp.bfloat16)
    grad_term = jnp.einsum("bac,abd->cd", flipped, pair_cotangent[0], preferred_element_type=jnp.float32)
    grad_flip = total(grad_term)

    flat = shared.reshape(-1, shared.shape[-1])
    key_rows, value_rows = flat[:, :key_dim], flat[:, key_dim : key_dim + value_dim]
    query_rows = queries.reshape(coarse * head_count, key_dim)
    scores = jnp.dot(query_rows, key_rows.T, preferred_element_type=jnp.float32)
    weights = jnp.exp(logit_cap * jnp.tanh(scores / logit_cap))
    totals = jnp.sum(weights, axis=-1, keepdims=True)
    mixed = jnp.dot(weights.astype(jnp.bfloat16), value_rows, preferred_element_type=jnp.float32) / totals
    heads_out = mixed.astype(jnp.bfloat16).reshape(coarse, head_count * value_dim)
    block_out = (widened + jnp.dot(heads_out, output_weight, preferred_element_type=jnp.float32)).astype(jnp.bfloat16)
    return (block_out[None], pair_out[None], grad_flip)


def solution(mesh):
    rows = P("dp", ("seq", "mp"), None)
    pair = P("dp", ("seq", "mp"), None, None)
    placed = (rows, P(None, ("seq", "mp"), None), P(), P(), P(), P(), P(), P(), pair, P(), pair)
    return jax.shard_map(per_device, mesh=mesh, in_specs=placed, out_specs=(rows, pair, P()), check_vma=False)
```

```python
import functools
import math

import jax
import jax.numpy as jnp
import numpy as np
from jax import lax
from jax.experimental import pallas as pl
from jax.experimental.pallas import tpu as pltpu
from jax.sharding import PartitionSpec as P

MESH = pl.DeviceIdType.MESH
PAIR_POOL = 16
SIDE = 4
CORES = 2
Z_LO = 4
norm_eps = 1e-06
logit_cap = 50.0


def root_norm(values_in):
    return values_in * lax.rsqrt(jnp.mean(values_in * values_in, axis=-1, keepdims=True) + norm_eps)


def prepare(raw):
    return jax.nn.gelu(root_norm(raw.astype(jnp.float32)), approximate=False).astype(jnp.bfloat16)


def rcopy(src, dst, ssem, rsem, dev):
    return pltpu.make_async_remote_copy(
        src_ref=src, dst_ref=dst, send_sem=ssem, recv_sem=rsem, device_id=dev, device_id_type=MESH
    )


class Gather:
    def __init__(self, buf, own_src, rows, cut, zsend, zrecv, ssem, rsem, lsem, mirror=False):
        self.mirror = mirror
        self.buf, self.own_src, self.rows, self.cut = buf, own_src, rows, cut
        self.zsend, self.zrecv, self.ssem, self.rsem, self.lsem = zsend, zrecv, ssem, rsem, lsem
        self.dp, self.seq, self.mp = (lax.axis_index(a) for a in ("dp", "seq", "mp"))
        self.x, self.y = self.seq // SIDE, self.seq % SIDE
        self.count = 0
        self.sent = []
        self.pending_local = []

    def z_partner(self):
        if not self.mirror:
            return {"mp": 1 - self.mp}
        core, z = self.dp % CORES, self.dp // CORES
        return {"dp": (Z_LO - 1 - z) * CORES + core, "mp": 1 - self.mp}

    def peers(self):
        out = [self.z_partner()]
        for q in (0, 1):
            for d in (1, -1):
                out.append({"seq": self.bid(q, d, 0)})
        return out

    def bid(self, q, da, db):
        first, second = (self.x, self.y) if q == 0 else (self.y, self.x)
        a, b = (first + da + SIDE) % SIDE, (second + db + SIDE) % SIDE
        return a * SIDE + b if q == 0 else b * SIDE + a

    def z_of(self, zsel):
        return self.mp if zsel == 0 else 1 - self.mp

    def view(self, q, zsel, da, db, half):
        ref = self.buf.at[q, self.z_of(zsel), self.bid(q, da, db)]
        if half == 0:
            return ref.at[pl.ds(0, self.cut)]
        if half == 1:
            return ref.at[pl.ds(self.cut, self.rows - self.cut)]
        return ref

    def sem(self, q, zsel, da, db, half):
        return self.rsem.at[q, self.z_of(zsel), self.bid(q, da, db), 1 if half == 1 else 0]

    def send(self, q, zsel, da, db, half, to, src=None):
        view = self.view(q, zsel, da, db, half)
        copy = rcopy(view if src is None else src, view, self.ssem.at[self.count],
                     self.sem(q, zsel, da, db, half), {"seq": self.bid(q, *to)})
        self.count += 1
        copy.start()
        self.sent.append(copy)

    def recv(self, q, zsel, da, db, half=None):
        view = self.view(q, zsel, da, db, half)
        rcopy(view, view, self.ssem.at[0], self.sem(q, zsel, da, db, half), {"seq": self.bid(q, 1, 0)}).wait_recv()

    def start_z(self):
        for q in (0, 1):
            copy = rcopy(self.own_src(q), self.view(q, 0, 0, 0, None), self.zsend.at[q], self.zrecv.at[q], self.z_partner())
            copy.start()
            self.sent.append(copy)
            local = pltpu.make_async_copy(self.own_src(q), self.view(q, 0, 0, 0, None), self.lsem.at[q])
            local.start()
            self.pending_local.append(local)

    def stage(self, q, zsel, n):
        if n == 0:
            src = self.own_src(q) if zsel == 0 else None
            if zsel == 1:
                view = self.view(q, 1, 0, 0, None)
                rcopy(view, view, self.zsend.at[q], self.zrecv.at[q], self.z_partner()).wait_recv()
            for to in ((1, 0), (-1, 0), (0, 1), (0, -1)):
                self.send(q, zsel, 0, 0, None, to, src)
        elif n in (1, 2):
            d = -1 if n == 1 else 1
            self.recv(q, zsel, d, 0)
            self.send(q, zsel, d, 0, 0 if n == 1 else 1, (-d, 0))
            for to in ((0, 1), (0, -1)):
                self.send(q, zsel, d, 0, None, to)
        elif n == 4:
            self.recv(q, zsel, 2, 0, 0)
            self.recv(q, zsel, 2, 0, 1)
            for to in ((0, 1), (0, -1)):
                self.send(q, zsel, 2, 0, None, to)
        elif n in (3, 5, 6, 7):
            da = {3: 0, 5: -1, 6: 1, 7: 2}[n]
            for d, half in ((-1, 0), (1, 1)):
                self.recv(q, zsel, da, d)
                self.send(q, zsel, da, d, half, (0, -d))
        else:
            for da in (0, -1, 1, 2):
                for half in (0, 1):
                    self.recv(q, zsel, da, 2, half)

    def drain(self):
        for copy in self.sent:
            copy.wait_send()


ORDER = [(0, 0), (0, 1), (0, 2), (0, 3), (1, 0), (0, 4), (0, 5), (0, 6), (1, 1), (1, 2), (0, 7), (1, 3), (1, 4), (1, 5), (1, 6), (1, 7)]
GATHER_SENDS = 80


def gather_sems():
    dma = pltpu.SemaphoreType.DMA
    return [dma((2,)), dma((2,)), dma((GATHER_SENDS,)), dma((2, 2, SIDE * SIDE, 2)), dma((2,))]


def greet(peers):
    barrier = pltpu.get_barrier_semaphore()
    for peer in peers:
        pl.semaphore_signal(barrier, inc=1, device_id=peer, device_id_type=MESH)
    pl.semaphore_wait(barrier, len(peers))


def conv_kernel(
    w_ref, prep_ref, edge_ref, skip_ref, chan_ref, enc_ref,
    F, X, P2, S2, H, acc, stage, zs, zr, ss, rs, ls, xs, xr,
):
    dp, seq, mp = (lax.axis_index(a) for a in ("dp", "seq", "mp"))
    core = dp % CORES
    other = dp - core + (1 - core)
    rows, cut = w_ref.shape[0], 112
    taps, depth = 5, rows // 5
    width = F.shape[4]

    def cols(n, count=1):
        return pl.ds(pl.multiple_of(n * width, width), count * width)

    g = Gather(F, lambda q: w_ref.at[:, cols(CORES * core + q)], rows, cut, zs, zr, ss, rs, ls, mirror=True)
    place = seq * 2 + mp
    last_place = SIDE * SIDE * 2 - 1
    after, before = (place + 1) % (last_place + 1), (place + last_place) % (last_place + 1)

    def at(p, d):
        return {"dp": d, "seq": p // 2, "mp": p % 2}

    partner = {"dp": other}
    greet(g.peers() + [partner, at(after, dp), at(after, other), at(before, dp), at(before, other)])

    g.start_z()
    extra = []
    n = 0
    for w, d in ((0, dp), (1, other)):
        extra.append(rcopy(edge_ref.at[1], H.at[w, 0], xs.at[n], xr.at[n], at(after, d)))
        extra.append(rcopy(edge_ref.at[0], H.at[w, 1], xs.at[n + 1], xr.at[n + 1], at(before, d)))
        n += 2
    extra.append(rcopy(prep_ref, P2, xs.at[4], xr.at[4], partner))
    extra.append(rcopy(skip_ref.at[:, cols(CORES * (1 - core), 2)], S2, xs.at[5], xr.at[5], partner))
    for copy in extra:
        copy.start()
    for q in (0, 1):
        g.stage(q, 0, 0)

    def spread(w, n):
        zabs, lanes = n // 3, pl.ds((n % 3) * 256, 256)
        chan = chan_ref[:, n * 256 : (n + 1) * 256]
        cin = prep_ref.shape[2]
        pick = (lax.broadcasted_iota(jnp.int32, (cin, 256), 0) == chan).astype(jnp.float32).astype(jnp.bfloat16)
        src = prep_ref if w == 0 else P2
        height = src.shape[1]
        dot = functools.partial(jnp.dot, preferred_element_type=jnp.float32)
        even, odd = dot(src[0], pick), dot(src[1], pick)
        prev, nxt = dot(H[w, 0], pick), dot(H[w, 1], pick)
        prev = jnp.where(place == 0, 0.0, prev)
        nxt = jnp.where(place == last_place, 0.0, nxt)
        row = lax.broadcasted_iota(jnp.int32, (height, 256), 0)
        for m, (arr, halo, shift) in enumerate((
            (even, prev[14:15], 1), (odd, prev[15:16], 1), (even, None, 0), (odd, None, 0),
            (even, nxt[0:1], -1), (odd, nxt[1:2], -1),
        )):
            if shift == 1:
                arr = jnp.where(row == 0, halo, pltpu.roll(arr, 1, 0))
            elif shift == -1:
                arr = jnp.where(row == height - 1, halo, pltpu.roll(arr, height - 1, 0))
            X[w, zabs, m, :, lanes] = arr.astype(jnp.bfloat16)

    def do_spread(k):
        w, n = divmod(k, 6)
        if k == 0:
            for copy in extra:
                copy.wait_recv()
        spread(w, n)

    todo = list(range(12))
    for i, (zsel, st) in enumerate(ORDER[1:]):
        if i >= 1 and todo:
            do_spread(todo.pop(0))
        for q in (0, 1):
            g.stage(q, zsel, st)
    while todo:
        do_spread(todo.pop(0))

    for local in g.pending_local:
        local.wait()

    def conv(zsel):
        za = g.z_of(zsel)
        for q in (0, 1):
            def tap(k, carry):
                lhs = X[:, za, pl.ds(k, 2)].reshape(acc.shape[1], -1)
                rhs = F[q, za, :, pl.ds(pl.multiple_of(k * depth, 16), depth), :].reshape(-1, width)
                acc[q] += jnp.dot(lhs, rhs, preferred_element_type=jnp.float32)
                return carry
            lax.fori_loop(0, taps, tap, 0)

    acc[...] = jnp.zeros_like(acc)
    for q in (0, 1):
        g.stage(q, 0, 8)
    conv(0)
    for q in (0, 1):
        g.stage(q, 1, 8)
    conv(1)
    half = acc.shape[1] // 2
    coarse = half // 2
    finals = []
    for q in (0, 1):
        total = acc[q, half:] + S2[:, q * width : (q + 1) * width].astype(jnp.float32)
        stage[q] = jnp.maximum(total[:coarse], total[coarse:]).astype(jnp.bfloat16)
        copy = rcopy(stage.at[q], enc_ref.at[:, cols(CORES * core + q)], xs.at[6 + q], xr.at[6 + q], partner)
        copy.start()
        finals.append(copy)
    for q in (0, 1):
        total = acc[q, :half] + skip_ref[:, cols(CORES * core + q)].astype(jnp.float32)
        enc_ref[:, cols(CORES * core + q)] = jnp.maximum(total[:coarse], total[coarse:]).astype(jnp.bfloat16)
    for q in (0, 1):
        view = enc_ref.at[:, cols(CORES * (1 - core) + q)]
        rcopy(stage.at[q], view, xs.at[6 + q], xr.at[6 + q], partner).wait_recv()
    g.drain()
    for copy in extra + finals:
        copy.wait_send()


def encode(filt, prep, edge, skip, chan):
    vm = pl.BlockSpec(memory_space=pltpu.VMEM)
    dma = pltpu.SemaphoreType.DMA
    rows, model_dim = filt.shape
    width = model_dim // 4
    coarse = prep.shape[1]
    kdepth = SIDE * SIDE * rows // 5
    return pl.pallas_call(
        conv_kernel,
        out_shape=jax.ShapeDtypeStruct((coarse, model_dim), jnp.bfloat16),
        in_specs=[vm] * 5,
        out_specs=vm,
        scratch_shapes=[
            pltpu.VMEM((2, 2, SIDE * SIDE, rows, width), jnp.bfloat16),
            pltpu.VMEM((2, 2, 6, coarse, kdepth), jnp.bfloat16),
            pltpu.VMEM(prep.shape, jnp.bfloat16),
            pltpu.VMEM((2 * coarse, 2 * width), jnp.bfloat16),
            pltpu.VMEM((2, 2, 16, prep.shape[2]), jnp.bfloat16),
            pltpu.VMEM((2, 4 * coarse, width), jnp.float32),
            pltpu.VMEM((2, coarse, width), jnp.bfloat16),
        ] + gather_sems() + [dma((8,)), dma((8,))],
        compiler_params=pltpu.CompilerParams(collective_id=0, has_side_effects=True, vmem_limit_bytes=60 << 20),
        name="encode",
    )(filt, prep, edge, skip, chan)


def share_kernel(src_ref, pair_ref, out_ref, turn_ref, zs, zr, ss, rs, ls, ts, tr):
    rows = src_ref.shape[1]
    g = Gather(out_ref, lambda q: src_ref.at[q], rows, rows // 2, zs, zr, ss, rs, ls)
    n = pair_ref.shape[0]
    place = g.seq * 2 + g.mp
    others = [(place + d) % n for d in range(1, n)]
    devices = [{"seq": p // 2, "mp": p % 2} for p in others]
    greet(devices)
    g.start_z()
    turns = [rcopy(pair_ref.at[p], turn_ref.at[place], ts.at[d], tr.at[place], devices[d]) for d, p in enumerate(others)]
    waiting = list(turns)
    turn_ref[place] = pair_ref[place]
    for zsel, st in ORDER + [(0, 8), (1, 8)]:
        for q in (0, 1):
            g.stage(q, zsel, st)
        for copy in waiting[:2]:
            copy.start()
        waiting = waiting[2:]
    for d, p in enumerate(others):
        view = turn_ref.at[p]
        rcopy(view, view, ts.at[d], tr.at[p], devices[d]).wait_recv()
    for local in g.pending_local:
        local.wait()
    g.drain()
    for copy in turns:
        copy.wait_send()


def share(src, pair):
    vm = pl.BlockSpec(memory_space=pltpu.VMEM)
    dma = pltpu.SemaphoreType.DMA
    return pl.pallas_call(
        share_kernel,
        out_shape=(
            jax.ShapeDtypeStruct((2, 2, SIDE * SIDE) + src.shape[1:], src.dtype),
            jax.ShapeDtypeStruct(pair.shape, pair.dtype),
        ),
        in_specs=[vm, vm],
        out_specs=(vm, vm),
        scratch_shapes=gather_sems() + [dma((pair.shape[0],))] * 2,
        compiler_params=pltpu.CompilerParams(collective_id=1, has_side_effects=True, vmem_limit_bytes=32 << 20),
        name="share",
    )(src, pair)


def total_kernel(g_ref, out_ref, R1, R2, fin, s1, r1, s2, r2, s3, r3):
    dp, seq, mp = (lax.axis_index(a) for a in ("dp", "seq", "mp"))
    n1, n2 = SIDE * SIDE, Z_LO * CORES * 2
    rows = g_ref.shape[0] // n1
    plane = [{"seq": (seq + d) % n1} for d in range(1, n1)]
    mine = dp * 2 + mp
    column = []
    for d in range(1, n2):
        t = (mine + d) % n2
        column.append({"dp": t // 2, "mp": t % 2})
    greet(plane + column)
    sent = []
    for d, dev in enumerate(plane):
        c = rcopy(g_ref.at[pl.ds(pl.multiple_of(dev["seq"] * rows, rows), rows)], R1.at[seq], s1.at[d], r1.at[seq], dev)
        c.start()
        sent.append(c)
    own = g_ref[pl.ds(pl.multiple_of(seq * rows, rows), rows)]
    R1[seq] = own
    for d, dev in enumerate(plane):
        view = R1.at[dev["seq"]]
        rcopy(view, view, s1.at[d], r1.at[dev["seq"]], dev).wait_recv()
    fin[0] = jnp.sum(R1[...], axis=0)
    for d, dev in enumerate(column):
        c = rcopy(fin.at[0], R2.at[mine], s2.at[d], r2.at[mine], dev)
        c.start()
        sent.append(c)
    R2[mine] = fin[0]
    for d, dev in enumerate(column):
        t = dev["dp"] * 2 + dev["mp"]
        rcopy(R2.at[t], R2.at[t], s2.at[d], r2.at[t], dev).wait_recv()
    fin[1] = jnp.sum(R2[...], axis=0)
    piece = pl.ds(pl.multiple_of(seq * rows, rows), rows)
    for d, dev in enumerate(plane):
        c = rcopy(fin.at[1], out_ref.at[piece], s3.at[d], r3.at[seq], dev)
        c.start()
        sent.append(c)
    out_ref[piece] = fin[1]
    for d, dev in enumerate(plane):
        view = out_ref.at[pl.ds(pl.multiple_of(dev["seq"] * rows, rows), rows)]
        rcopy(view, view, s3.at[d], r3.at[dev["seq"]], dev).wait_recv()
    for c in sent:
        c.wait_send()


def total(term):
    vm = pl.BlockSpec(memory_space=pltpu.VMEM)
    dma = pltpu.SemaphoreType.DMA
    rows = term.shape[0] // (SIDE * SIDE)
    n = SIDE * SIDE
    block = (n, rows, term.shape[1])
    return pl.pallas_call(
        total_kernel,
        out_shape=jax.ShapeDtypeStruct(term.shape, term.dtype),
        in_specs=[vm],
        out_specs=vm,
        scratch_shapes=[pltpu.VMEM(block, jnp.float32), pltpu.VMEM(block, jnp.float32), pltpu.VMEM((2,) + block[1:], jnp.float32)]
        + [dma((n,))] * 6,
        compiler_params=pltpu.CompilerParams(collective_id=2, has_side_effects=True, vmem_limit_bytes=16 << 20),
        name="total",
    )(term)


def per_device(
    features, conv_weight, norm_gain, query_weight, keyval_weight, head_scale, output_weight, pair_weight,
    pair_input, flip_weight, pair_cotangent,
):
    fine_rows, in_channels = features.shape[1:]
    coarse = fine_rows // 2
    model_dim = output_weight.shape[1]
    head_count = head_scale.shape[0]
    key_dim = query_weight.shape[1] // head_count
    value_dim = keyval_weight.shape[1] - key_dim
    pair_dim = flip_weight.shape[0]
    taps, per_shard = conv_weight.shape[:2]
    padded = 48

    filt = jnp.pad(conv_weight, ((0, 0), (0, padded - per_shard), (0, 0))).reshape(taps * padded, model_dim)
    prepared = prepare(features[0])
    edge = jnp.stack([prepared[:16], prepared[fine_rows - 16 :]])
    wanted = np.arange(fine_rows).reshape(coarse, 2).T.reshape(-1)
    split = (jnp.asarray(wanted.astype(np.int32))[:, None] == lax.broadcasted_iota(jnp.int32, (1, fine_rows), 1)).astype(jnp.bfloat16)
    prep = jnp.dot(split, prepared, preferred_element_type=jnp.float32).astype(jnp.bfloat16)
    prep = prep.reshape(2, coarse, in_channels)
    skip = jnp.dot(split, features[0], preferred_element_type=jnp.float32).astype(jnp.bfloat16)
    skip = jnp.pad(skip, ((0, 0), (0, model_dim - in_channels)))
    lane = np.arange(2 * SIDE * SIDE * padded)
    zh, sq, ch = lane // (SIDE * SIDE * padded), (lane // padded) % (SIDE * SIDE), lane % padded
    chan = np.where(ch < per_shard, per_shard * (2 * sq + zh) + ch, -1).astype(np.int32)[None]
    encoded = encode(filt, prep, edge, skip, jnp.asarray(chan))

    widened = encoded.astype(jnp.float32)
    normed = (root_norm(widened) * norm_gain).astype(jnp.bfloat16)
    keyvals = jnp.dot(normed, keyval_weight, preferred_element_type=jnp.float32).astype(jnp.bfloat16)
    pooled = jnp.mean(widened.reshape(coarse // PAIR_POOL, PAIR_POOL, model_dim), axis=1).astype(jnp.bfloat16)
    feats = jnp.dot(pooled, pair_weight, preferred_element_type=jnp.float32).astype(jnp.bfloat16)
    pair_rows = feats.shape[0]
    spare = jnp.pad(feats.reshape(-1, 64), ((0, coarse - feats.size // 64), (0, 0)))
    block = jnp.concatenate([keyvals, spare], axis=1).reshape(2, coarse // 2, -1)
    blocks = 2 * SIDE * SIDE
    pieces = pair_input[0].reshape(pair_rows, blocks, -1, pair_dim).transpose(1, 0, 2, 3)
    shared, turned_in = share(block, pieces.reshape(blocks, -1, pair_dim))
    turned_in = turned_in.reshape(blocks * pair_rows, -1, pair_dim)
    scale_row = jnp.repeat(head_scale, key_dim) / math.sqrt(key_dim)
    queries = (jnp.dot(normed, query_weight, preferred_element_type=jnp.float32) * scale_row).astype(jnp.bfloat16)

    feats_all = shared[0, :, :, : feats.size // 64, key_dim + value_dim :]
    feats_all = feats_all.transpose(1, 0, 2, 3).reshape(-1, 2 * pair_dim).astype(jnp.float32)
    pair_q, pair_k = feats[:, :pair_dim].astype(jnp.float32), feats[:, pair_dim:].astype(jnp.float32)
    q_all, k_all = feats_all[:, :pair_dim], feats_all[:, pair_dim:]
    summed = (pair_input[0].astype(jnp.float32) + pair_q[:, None, :] * k_all[None]).astype(jnp.bfloat16)
    flipped = (turned_in.astype(jnp.float32) + q_all[:, None, :] * pair_k[None]).astype(jnp.bfloat16)
    turned = jnp.einsum("bac,cd->abd", flipped, flip_weight, preferred_element_type=jnp.float32)
    pair_out = (summed.astype(jnp.float32) + turned).astype(jnp.bfloat16)
    grad_term = jnp.einsum("bac,abd->cd", flipped, pair_cotangent[0], preferred_element_type=jnp.float32)
    grad_flip = total(grad_term)

    flat = shared.reshape(-1, shared.shape[-1])
    key_rows, value_rows = flat[:, :key_dim], flat[:, key_dim : key_dim + value_dim]
    query_rows = queries.reshape(coarse * head_count, key_dim)
    scores = jnp.dot(query_rows, key_rows.T, preferred_element_type=jnp.float32)
    weights = jnp.exp(logit_cap * jnp.tanh(scores / logit_cap))
    totals = jnp.sum(weights, axis=-1, keepdims=True)
    mixed = jnp.dot(weights.astype(jnp.bfloat16), value_rows, preferred_element_type=jnp.float32) / totals
    heads_out = mixed.astype(jnp.bfloat16).reshape(coarse, head_count * value_dim)
    block_out = (widened + jnp.dot(heads_out, output_weight, preferred_element_type=jnp.float32)).astype(jnp.bfloat16)
    return (block_out[None], pair_out[None], grad_flip)


def solution(mesh):
    rows = P("dp", ("seq", "mp"), None)
    pair = P("dp", ("seq", "mp"), None, None)
    placed = (rows, P(None, ("seq", "mp"), None), P(), P(), P(), P(), P(), P(), pair, P(), pair)
    return jax.shard_map(per_device, mesh=mesh, in_specs=placed, out_specs=(rows, pair, P()), check_vma=False)
```

```python
import functools
import math

import jax
import jax.numpy as jnp
import numpy as np
from jax import lax
from jax.experimental import pallas as pl
from jax.experimental.pallas import tpu as pltpu
from jax.sharding import PartitionSpec as P

MESH = pl.DeviceIdType.MESH
PAIR_POOL = 16
SIDE = 4
CORES = 2
Z_LO = 4
norm_eps = 1e-06
logit_cap = 50.0


def root_norm(values_in):
    return values_in * lax.rsqrt(jnp.mean(values_in * values_in, axis=-1, keepdims=True) + norm_eps)


def prepare(raw):
    return jax.nn.gelu(root_norm(raw.astype(jnp.float32)), approximate=False).astype(jnp.bfloat16)


def rcopy(src, dst, ssem, rsem, dev):
    return pltpu.make_async_remote_copy(
        src_ref=src, dst_ref=dst, send_sem=ssem, recv_sem=rsem, device_id=dev, device_id_type=MESH
    )


class Gather:
    def __init__(self, buf, own_src, rows, cut, zsend, zrecv, ssem, rsem, lsem, mirror=False):
        self.mirror = mirror
        self.buf, self.own_src, self.rows, self.cut = buf, own_src, rows, cut
        self.zsend, self.zrecv, self.ssem, self.rsem, self.lsem = zsend, zrecv, ssem, rsem, lsem
        self.dp, self.seq, self.mp = (lax.axis_index(a) for a in ("dp", "seq", "mp"))
        self.x, self.y = self.seq // SIDE, self.seq % SIDE
        self.count = 0
        self.sent = []
        self.pending_local = []

    def z_partner(self):
        if not self.mirror:
            return {"mp": 1 - self.mp}
        core, z = self.dp % CORES, self.dp // CORES
        return {"dp": (Z_LO - 1 - z) * CORES + core, "mp": 1 - self.mp}

    def peers(self):
        out = [self.z_partner()]
        for q in (0, 1):
            for d in (1, -1):
                out.append({"seq": self.bid(q, d, 0)})
        return out

    def bid(self, q, da, db):
        first, second = (self.x, self.y) if q == 0 else (self.y, self.x)
        a, b = (first + da + SIDE) % SIDE, (second + db + SIDE) % SIDE
        return a * SIDE + b if q == 0 else b * SIDE + a

    def z_of(self, zsel):
        return self.mp if zsel == 0 else 1 - self.mp

    def view(self, q, zsel, da, db, half):
        ref = self.buf.at[q, self.z_of(zsel), self.bid(q, da, db)]
        if half == 0:
            return ref.at[pl.ds(0, self.cut)]
        if half == 1:
            return ref.at[pl.ds(self.cut, self.rows - self.cut)]
        return ref

    def sem(self, q, zsel, da, db, half):
        return self.rsem.at[q, self.z_of(zsel), self.bid(q, da, db), 1 if half == 1 else 0]

    def send(self, q, zsel, da, db, half, to, src=None):
        view = self.view(q, zsel, da, db, half)
        copy = rcopy(view if src is None else src, view, self.ssem.at[self.count],
                     self.sem(q, zsel, da, db, half), {"seq": self.bid(q, *to)})
        self.count += 1
        copy.start()
        self.sent.append(copy)

    def recv(self, q, zsel, da, db, half=None):
        view = self.view(q, zsel, da, db, half)
        rcopy(view, view, self.ssem.at[0], self.sem(q, zsel, da, db, half), {"seq": self.bid(q, 1, 0)}).wait_recv()

    def start_z(self):
        for q in (0, 1):
            copy = rcopy(self.own_src(q), self.view(q, 0, 0, 0, None), self.zsend.at[q], self.zrecv.at[q], self.z_partner())
            copy.start()
            self.sent.append(copy)
            local = pltpu.make_async_copy(self.own_src(q), self.view(q, 0, 0, 0, None), self.lsem.at[q])
            local.start()
            self.pending_local.append(local)

    def stage(self, q, zsel, n):
        if n == 0:
            src = self.own_src(q) if zsel == 0 else None
            if zsel == 1:
                view = self.view(q, 1, 0, 0, None)
                rcopy(view, view, self.zsend.at[q], self.zrecv.at[q], self.z_partner()).wait_recv()
            for to in ((1, 0), (-1, 0), (0, 1), (0, -1)):
                self.send(q, zsel, 0, 0, None, to, src)
        elif n in (1, 2):
            d = -1 if n == 1 else 1
            self.recv(q, zsel, d, 0)
            self.send(q, zsel, d, 0, 0 if n == 1 else 1, (-d, 0))
            for to in ((0, 1), (0, -1)):
                self.send(q, zsel, d, 0, None, to)
        elif n == 4:
            self.recv(q, zsel, 2, 0, 0)
            self.recv(q, zsel, 2, 0, 1)
            for to in ((0, 1), (0, -1)):
                self.send(q, zsel, 2, 0, None, to)
        elif n in (3, 5, 6, 7):
            da = {3: 0, 5: -1, 6: 1, 7: 2}[n]
            for d, half in ((-1, 0), (1, 1)):
                self.recv(q, zsel, da, d)
                self.send(q, zsel, da, d, half, (0, -d))
        else:
            for da in (0, -1, 1, 2):
                for half in (0, 1):
                    self.recv(q, zsel, da, 2, half)

    def drain(self):
        for copy in self.sent:
            copy.wait_send()


ORDER = [(0, 0), (0, 1), (0, 2), (0, 3), (1, 0), (0, 4), (0, 5), (0, 6), (1, 1), (1, 2), (0, 7), (1, 3), (1, 4), (1, 5), (1, 6), (1, 7)]
GATHER_SENDS = 80


def gather_sems():
    dma = pltpu.SemaphoreType.DMA
    return [dma((2,)), dma((2,)), dma((GATHER_SENDS,)), dma((2, 2, SIDE * SIDE, 2)), dma((2,))]


def greet(peers):
    barrier = pltpu.get_barrier_semaphore()
    for peer in peers:
        pl.semaphore_signal(barrier, inc=1, device_id=peer, device_id_type=MESH)
    pl.semaphore_wait(barrier, len(peers))


def conv_kernel(
    w_ref, prep_ref, edge_ref, skip_ref, chan_ref, enc_ref,
    F, X, P2, S2, H, acc, stage, zs, zr, ss, rs, ls, xs, xr,
):
    dp, seq, mp = (lax.axis_index(a) for a in ("dp", "seq", "mp"))
    core = dp % CORES
    other = dp - core + (1 - core)
    rows, cut = w_ref.shape[0], 112
    taps, depth = 5, rows // 5
    width = F.shape[4]

    def cols(n, count=1):
        return pl.ds(pl.multiple_of(n * width, width), count * width)

    g = Gather(F, lambda q: w_ref.at[:, cols(CORES * core + q)], rows, cut, zs, zr, ss, rs, ls, mirror=True)
    place = seq * 2 + mp
    last_place = SIDE * SIDE * 2 - 1
    after, before = (place + 1) % (last_place + 1), (place + last_place) % (last_place + 1)

    def at(p, d):
        return {"dp": d, "seq": p // 2, "mp": p % 2}

    partner = {"dp": other}
    greet(g.peers() + [partner, at(after, dp), at(after, other), at(before, dp), at(before, other)])

    g.start_z()
    extra = []
    n = 0
    for w, d in ((0, dp), (1, other)):
        extra.append(rcopy(edge_ref.at[1], H.at[w, 0], xs.at[n], xr.at[n], at(after, d)))
        extra.append(rcopy(edge_ref.at[0], H.at[w, 1], xs.at[n + 1], xr.at[n + 1], at(before, d)))
        n += 2
    extra.append(rcopy(prep_ref, P2, xs.at[4], xr.at[4], partner))
    extra.append(rcopy(skip_ref.at[:, cols(CORES * (1 - core), 2)], S2, xs.at[5], xr.at[5], partner))
    for copy in extra:
        copy.start()
    for q in (0, 1):
        g.stage(q, 0, 0)

    def spread(w, n):
        zabs, lanes = n // 3, pl.ds((n % 3) * 256, 256)
        chan = chan_ref[:, n * 256 : (n + 1) * 256]
        cin = prep_ref.shape[2]
        pick = (lax.broadcasted_iota(jnp.int32, (cin, 256), 0) == chan).astype(jnp.float32).astype(jnp.bfloat16)
        src = prep_ref if w == 0 else P2
        height = src.shape[1]
        dot = functools.partial(jnp.dot, preferred_element_type=jnp.float32)
        even, odd = dot(src[0], pick), dot(src[1], pick)
        prev, nxt = dot(H[w, 0], pick), dot(H[w, 1], pick)
        prev = jnp.where(place == 0, 0.0, prev)
        nxt = jnp.where(place == last_place, 0.0, nxt)
        row = lax.broadcasted_iota(jnp.int32, (height, 256), 0)
        for m, (arr, halo, shift) in enumerate((
            (even, prev[14:15], 1), (odd, prev[15:16], 1), (even, None, 0), (odd, None, 0),
            (even, nxt[0:1], -1), (odd, nxt[1:2], -1),
        )):
            if shift == 1:
                arr = jnp.where(row == 0, halo, pltpu.roll(arr, 1, 0))
            elif shift == -1:
                arr = jnp.where(row == height - 1, halo, pltpu.roll(arr, height - 1, 0))
            X[w, zabs, m, :, lanes] = arr.astype(jnp.bfloat16)

    def do_spread(k):
        w, n = divmod(k, 6)
        if k == 0:
            for copy in extra:
                copy.wait_recv()
        spread(w, n)

    todo = list(range(12))
    for i, (zsel, st) in enumerate(ORDER[1:]):
        if i >= 1 and todo:
            do_spread(todo.pop(0))
        for q in (0, 1):
            g.stage(q, zsel, st)
    while todo:
        do_spread(todo.pop(0))

    for local in g.pending_local:
        local.wait()

    def conv(zsel):
        za = g.z_of(zsel)
        for q in (0, 1):
            def tap(k, carry):
                lhs = X[:, za, pl.ds(k, 2)].reshape(acc.shape[1], -1)
                rhs = F[q, za, :, pl.ds(pl.multiple_of(k * depth, 16), depth), :].reshape(-1, width)
                acc[q] += jnp.dot(lhs, rhs, preferred_element_type=jnp.float32)
                return carry
            lax.fori_loop(0, taps, tap, 0)

    acc[...] = jnp.zeros_like(acc)
    for q in (0, 1):
        g.stage(q, 0, 8)
    conv(0)
    for q in (0, 1):
        g.stage(q, 1, 8)
    conv(1)
    half = acc.shape[1] // 2
    coarse = half // 2
    finals = []
    for q in (0, 1):
        total = acc[q, half:] + S2[:, q * width : (q + 1) * width].astype(jnp.float32)
        stage[q] = jnp.maximum(total[:coarse], total[coarse:]).astype(jnp.bfloat16)
        copy = rcopy(stage.at[q], enc_ref.at[:, cols(CORES * core + q)], xs.at[6 + q], xr.at[6 + q], partner)
        copy.start()
        finals.append(copy)
    for q in (0, 1):
        total = acc[q, :half] + skip_ref[:, cols(CORES * core + q)].astype(jnp.float32)
        enc_ref[:, cols(CORES * core + q)] = jnp.maximum(total[:coarse], total[coarse:]).astype(jnp.bfloat16)
    for q in (0, 1):
        view = enc_ref.at[:, cols(CORES * (1 - core) + q)]
        rcopy(stage.at[q], view, xs.at[6 + q], xr.at[6 + q], partner).wait_recv()
    g.drain()
    for copy in extra + finals:
        copy.wait_send()


def encode(filt, prep, edge, skip, chan):
    vm = pl.BlockSpec(memory_space=pltpu.VMEM)
    dma = pltpu.SemaphoreType.DMA
    rows, model_dim = filt.shape
    width = model_dim // 4
    coarse = prep.shape[1]
    kdepth = SIDE * SIDE * rows // 5
    return pl.pallas_call(
        conv_kernel,
        out_shape=jax.ShapeDtypeStruct((coarse, model_dim), jnp.bfloat16),
        in_specs=[vm] * 5,
        out_specs=vm,
        scratch_shapes=[
            pltpu.VMEM((2, 2, SIDE * SIDE, rows, width), jnp.bfloat16),
            pltpu.VMEM((2, 2, 6, coarse, kdepth), jnp.bfloat16),
            pltpu.VMEM(prep.shape, jnp.bfloat16),
            pltpu.VMEM((2 * coarse, 2 * width), jnp.bfloat16),
            pltpu.VMEM((2, 2, 16, prep.shape[2]), jnp.bfloat16),
            pltpu.VMEM((2, 4 * coarse, width), jnp.float32),
            pltpu.VMEM((2, coarse, width), jnp.bfloat16),
        ] + gather_sems() + [dma((8,)), dma((8,))],
        compiler_params=pltpu.CompilerParams(collective_id=0, has_side_effects=True, vmem_limit_bytes=60 << 20),
        name="encode",
    )(filt, prep, edge, skip, chan)


def share_kernel(src_ref, pair_ref, out_ref, turn_ref, zs, zr, ss, rs, ls, ts, tr):
    rows = src_ref.shape[1]
    g = Gather(out_ref, lambda q: src_ref.at[q], rows, rows // 2, zs, zr, ss, rs, ls)
    n = pair_ref.shape[0]
    place = g.seq * 2 + g.mp
    others = [(place + d) % n for d in range(1, n)]
    devices = [{"seq": p // 2, "mp": p % 2} for p in others]
    greet(devices)
    g.start_z()
    turns = [rcopy(pair_ref.at[p], turn_ref.at[place], ts.at[d], tr.at[place], devices[d]) for d, p in enumerate(others)]
    waiting = list(turns)
    turn_ref[place] = pair_ref[place]
    for zsel, st in ORDER + [(0, 8), (1, 8)]:
        for q in (0, 1):
            g.stage(q, zsel, st)
        for copy in waiting[:2]:
            copy.start()
        waiting = waiting[2:]
    for d, p in enumerate(others):
        view = turn_ref.at[p]
        rcopy(view, view, ts.at[d], tr.at[p], devices[d]).wait_recv()
    for local in g.pending_local:
        local.wait()
    g.drain()
    for copy in turns:
        copy.wait_send()


def share(src, pair):
    vm = pl.BlockSpec(memory_space=pltpu.VMEM)
    dma = pltpu.SemaphoreType.DMA
    return pl.pallas_call(
        share_kernel,
        out_shape=(
            jax.ShapeDtypeStruct((2, 2, SIDE * SIDE) + src.shape[1:], src.dtype),
            jax.ShapeDtypeStruct(pair.shape, pair.dtype),
        ),
        in_specs=[vm, vm],
        out_specs=(vm, vm),
        scratch_shapes=gather_sems() + [dma((pair.shape[0],))] * 2,
        compiler_params=pltpu.CompilerParams(collective_id=1, has_side_effects=True, vmem_limit_bytes=32 << 20),
        name="share",
    )(src, pair)


def attend_kernel(g_ref, q_ref, kv_ref, out_ref, mix_ref, R1, R2, fin, s1, r1, s2, r2, s3, r3, key_dim, value_dim):
    dp, seq, mp = (lax.axis_index(a) for a in ("dp", "seq", "mp"))

    def attend(first, end):
        def two(p, carry):
            mixes = []
            for e in (0, 1):
                query = q_ref[:, pl.ds(pl.multiple_of((2 * p + e) * key_dim, key_dim), key_dim)]
                mixed, norm = 0.0, 0.0
                for c in range(4):
                    keys = kv_ref[c // 2, c % 2, :, :, :key_dim].reshape(-1, key_dim)
                    values = kv_ref[c // 2, c % 2, :, :, key_dim : key_dim + value_dim].reshape(-1, value_dim)
                    score = lax.dot_general(query, keys, (((1,), (1,)), ((), ())), preferred_element_type=jnp.float32)
                    weight = jnp.exp(logit_cap * jnp.tanh(score * (1.0 / logit_cap)))
                    norm += jnp.sum(weight, axis=-1, keepdims=True)
                    mixed += jnp.dot(weight.astype(jnp.bfloat16), values, preferred_element_type=jnp.float32)
                mixes.append(mixed / norm)
            both = jnp.concatenate(mixes, axis=1).astype(jnp.bfloat16)
            mix_ref[:, pl.ds(pl.multiple_of(p * 2 * value_dim, 2 * value_dim), 2 * value_dim)] = both
            return carry
        lax.fori_loop(first, end, two, 0)

    n1, n2 = SIDE * SIDE, Z_LO * CORES * 2
    rows = g_ref.shape[0] // n1
    plane = [{"seq": (seq + d) % n1} for d in range(1, n1)]
    mine = dp * 2 + mp
    column = []
    for d in range(1, n2):
        t = (mine + d) % n2
        column.append({"dp": t // 2, "mp": t % 2})
    greet(plane + column)
    sent = []
    for d, dev in enumerate(plane):
        c = rcopy(g_ref.at[pl.ds(pl.multiple_of(dev["seq"] * rows, rows), rows)], R1.at[seq], s1.at[d], r1.at[seq], dev)
        c.start()
        sent.append(c)
    own = g_ref[pl.ds(pl.multiple_of(seq * rows, rows), rows)]
    R1[seq] = own
    attend(0, 1)
    for d, dev in enumerate(plane):
        view = R1.at[dev["seq"]]
        rcopy(view, view, s1.at[d], r1.at[dev["seq"]], dev).wait_recv()
    fin[0] = jnp.sum(R1[...], axis=0)
    for d, dev in enumerate(column):
        c = rcopy(fin.at[0], R2.at[mine], s2.at[d], r2.at[mine], dev)
        c.start()
        sent.append(c)
    R2[mine] = fin[0]
    attend(1, 2)
    for d, dev in enumerate(column):
        t = dev["dp"] * 2 + dev["mp"]
        rcopy(R2.at[t], R2.at[t], s2.at[d], r2.at[t], dev).wait_recv()
    fin[1] = jnp.sum(R2[...], axis=0)
    piece = pl.ds(pl.multiple_of(seq * rows, rows), rows)
    for d, dev in enumerate(plane):
        c = rcopy(fin.at[1], out_ref.at[piece], s3.at[d], r3.at[seq], dev)
        c.start()
        sent.append(c)
    out_ref[piece] = fin[1]
    attend(2, q_ref.shape[1] // key_dim // 2)
    for d, dev in enumerate(plane):
        view = out_ref.at[pl.ds(pl.multiple_of(dev["seq"] * rows, rows), rows)]
        rcopy(view, view, s3.at[d], r3.at[dev["seq"]], dev).wait_recv()
    for c in sent:
        c.wait_send()


def attend_and_total(term, queries, shared, key_dim, value_dim):
    vm = pl.BlockSpec(memory_space=pltpu.VMEM)
    dma = pltpu.SemaphoreType.DMA
    rows = term.shape[0] // (SIDE * SIDE)
    n = SIDE * SIDE
    block = (n, rows, term.shape[1])
    mixed = (queries.shape[0], queries.shape[1] // key_dim * value_dim)
    return pl.pallas_call(
        functools.partial(attend_kernel, key_dim=key_dim, value_dim=value_dim),
        out_shape=(jax.ShapeDtypeStruct(term.shape, term.dtype), jax.ShapeDtypeStruct(mixed, jnp.bfloat16)),
        in_specs=[vm] * 3,
        out_specs=(vm, vm),
        scratch_shapes=[pltpu.VMEM(block, jnp.float32), pltpu.VMEM(block, jnp.float32), pltpu.VMEM((2,) + block[1:], jnp.float32)]
        + [dma((n,))] * 6,
        compiler_params=pltpu.CompilerParams(collective_id=2, has_side_effects=True, vmem_limit_bytes=40 << 20),
        name="attend",
    )(term, queries, shared)


def per_device(
    features, conv_weight, norm_gain, query_weight, keyval_weight, head_scale, output_weight, pair_weight,
    pair_input, flip_weight, pair_cotangent,
):
    fine_rows, in_channels = features.shape[1:]
    coarse = fine_rows // 2
    model_dim = output_weight.shape[1]
    key_dim = query_weight.shape[1] // head_scale.shape[0]
    value_dim = keyval_weight.shape[1] - key_dim
    pair_dim = flip_weight.shape[0]
    taps, per_shard = conv_weight.shape[:2]
    padded = 48

    filt = jnp.pad(conv_weight, ((0, 0), (0, padded - per_shard), (0, 0))).reshape(taps * padded, model_dim)
    prepared = prepare(features[0])
    edge = jnp.stack([prepared[:16], prepared[fine_rows - 16 :]])
    wanted = np.arange(fine_rows).reshape(coarse, 2).T.reshape(-1)
    split = (jnp.asarray(wanted.astype(np.int32))[:, None] == lax.broadcasted_iota(jnp.int32, (1, fine_rows), 1)).astype(jnp.bfloat16)
    prep = jnp.dot(split, prepared, preferred_element_type=jnp.float32).astype(jnp.bfloat16)
    prep = prep.reshape(2, coarse, in_channels)
    skip = jnp.dot(split, features[0], preferred_element_type=jnp.float32).astype(jnp.bfloat16)
    skip = jnp.pad(skip, ((0, 0), (0, model_dim - in_channels)))
    lane = np.arange(2 * SIDE * SIDE * padded)
    zh, sq, ch = lane // (SIDE * SIDE * padded), (lane // padded) % (SIDE * SIDE), lane % padded
    chan = np.where(ch < per_shard, per_shard * (2 * sq + zh) + ch, -1).astype(np.int32)[None]
    encoded = encode(filt, prep, edge, skip, jnp.asarray(chan))

    widened = encoded.astype(jnp.float32)
    normed = (root_norm(widened) * norm_gain).astype(jnp.bfloat16)
    keyvals = jnp.dot(normed, keyval_weight, preferred_element_type=jnp.float32).astype(jnp.bfloat16)
    pooled = jnp.mean(widened.reshape(coarse // PAIR_POOL, PAIR_POOL, model_dim), axis=1).astype(jnp.bfloat16)
    feats = jnp.dot(pooled, pair_weight, preferred_element_type=jnp.float32).astype(jnp.bfloat16)
    pair_rows = feats.shape[0]
    spare = jnp.pad(feats.reshape(-1, 64), ((0, coarse - feats.size // 64), (0, 0)))
    block = jnp.concatenate([keyvals, spare], axis=1).reshape(2, coarse // 2, -1)
    blocks = 2 * SIDE * SIDE
    pieces = pair_input[0].reshape(pair_rows, blocks, -1, pair_dim).transpose(1, 0, 2, 3)
    shared, turned_in = share(block, pieces.reshape(blocks, -1, pair_dim))
    turned_in = turned_in.reshape(blocks * pair_rows, -1, pair_dim)
    scale_row = jnp.repeat(head_scale, key_dim) / math.sqrt(key_dim)
    queries = (jnp.dot(normed, query_weight, preferred_element_type=jnp.float32) * scale_row).astype(jnp.bfloat16)

    feats_all = shared[0, :, :, : feats.size // 64, key_dim + value_dim :]
    feats_all = feats_all.transpose(1, 0, 2, 3).reshape(-1, 2 * pair_dim).astype(jnp.float32)
    pair_q, pair_k = feats[:, :pair_dim].astype(jnp.float32), feats[:, pair_dim:].astype(jnp.float32)
    q_all, k_all = feats_all[:, :pair_dim], feats_all[:, pair_dim:]
    summed = (pair_input[0].astype(jnp.float32) + pair_q[:, None, :] * k_all[None]).astype(jnp.bfloat16)
    flipped = (turned_in.astype(jnp.float32) + q_all[:, None, :] * pair_k[None]).astype(jnp.bfloat16)
    turned = jnp.einsum("bac,cd->abd", flipped, flip_weight, preferred_element_type=jnp.float32)
    pair_out = (summed.astype(jnp.float32) + turned).astype(jnp.bfloat16)
    grad_term = jnp.einsum("bac,abd->cd", flipped, pair_cotangent[0], preferred_element_type=jnp.float32)
    grad_flip, heads_out = attend_and_total(grad_term, queries, shared, key_dim, value_dim)

    block_out = (widened + jnp.dot(heads_out, output_weight, preferred_element_type=jnp.float32)).astype(jnp.bfloat16)
    return (block_out[None], pair_out[None], grad_flip)


def solution(mesh):
    rows = P("dp", ("seq", "mp"), None)
    pair = P("dp", ("seq", "mp"), None, None)
    placed = (rows, P(None, ("seq", "mp"), None), P(), P(), P(), P(), P(), P(), pair, P(), pair)
    return jax.shard_map(per_device, mesh=mesh, in_specs=placed, out_specs=(rows, pair, P()), check_vma=False)
```

```python
import functools
import math

import jax
import jax.numpy as jnp
import numpy as np
from jax import lax
from jax.experimental import pallas as pl
from jax.experimental.pallas import tpu as pltpu
from jax.sharding import PartitionSpec as P

MESH = pl.DeviceIdType.MESH
PAIR_POOL = 16
SIDE = 4
CORES = 2
Z_LO = 4
norm_eps = 1e-06
logit_cap = 50.0


def root_norm(values_in):
    return values_in * lax.rsqrt(jnp.mean(values_in * values_in, axis=-1, keepdims=True) + norm_eps)


def prepare(raw):
    return jax.nn.gelu(root_norm(raw.astype(jnp.float32)), approximate=False).astype(jnp.bfloat16)


def rcopy(src, dst, ssem, rsem, dev):
    return pltpu.make_async_remote_copy(
        src_ref=src, dst_ref=dst, send_sem=ssem, recv_sem=rsem, device_id=dev, device_id_type=MESH
    )


class Gather:
    def __init__(self, buf, own_src, rows, cut, zsend, zrecv, ssem, rsem, lsem, mirror=False):
        self.mirror = mirror
        self.buf, self.own_src, self.rows, self.cut = buf, own_src, rows, cut
        self.zsend, self.zrecv, self.ssem, self.rsem, self.lsem = zsend, zrecv, ssem, rsem, lsem
        self.dp, self.seq, self.mp = (lax.axis_index(a) for a in ("dp", "seq", "mp"))
        self.x, self.y = self.seq // SIDE, self.seq % SIDE
        self.count = 0
        self.sent = []
        self.pending_local = []

    def z_partner(self):
        if not self.mirror:
            return {"mp": 1 - self.mp}
        core, z = self.dp % CORES, self.dp // CORES
        return {"dp": (Z_LO - 1 - z) * CORES + core, "mp": 1 - self.mp}

    def peers(self):
        out = [self.z_partner()]
        for q in (0, 1):
            for d in (1, -1):
                out.append({"seq": self.bid(q, d, 0)})
        return out

    def bid(self, q, da, db):
        first, second = (self.x, self.y) if q == 0 else (self.y, self.x)
        a, b = (first + da + SIDE) % SIDE, (second + db + SIDE) % SIDE
        return a * SIDE + b if q == 0 else b * SIDE + a

    def z_of(self, zsel):
        return self.mp if zsel == 0 else 1 - self.mp

    def view(self, q, zsel, da, db, half):
        ref = self.buf.at[q, self.z_of(zsel), self.bid(q, da, db)]
        if half == 0:
            return ref.at[pl.ds(0, self.cut)]
        if half == 1:
            return ref.at[pl.ds(self.cut, self.rows - self.cut)]
        return ref

    def sem(self, q, zsel, da, db, half):
        return self.rsem.at[q, self.z_of(zsel), self.bid(q, da, db), 1 if half == 1 else 0]

    def send(self, q, zsel, da, db, half, to, src=None):
        view = self.view(q, zsel, da, db, half)
        copy = rcopy(view if src is None else src, view, self.ssem.at[self.count],
                     self.sem(q, zsel, da, db, half), {"seq": self.bid(q, *to)})
        self.count += 1
        copy.start()
        self.sent.append(copy)

    def recv(self, q, zsel, da, db, half=None):
        view = self.view(q, zsel, da, db, half)
        rcopy(view, view, self.ssem.at[0], self.sem(q, zsel, da, db, half), {"seq": self.bid(q, 1, 0)}).wait_recv()

    def start_z(self):
        for q in (0, 1):
            copy = rcopy(self.own_src(q), self.view(q, 0, 0, 0, None), self.zsend.at[q], self.zrecv.at[q], self.z_partner())
            copy.start()
            self.sent.append(copy)
            local = pltpu.make_async_copy(self.own_src(q), self.view(q, 0, 0, 0, None), self.lsem.at[q])
            local.start()
            self.pending_local.append(local)

    def stage(self, q, zsel, n):
        if n == 0:
            src = self.own_src(q) if zsel == 0 else None
            if zsel == 1:
                view = self.view(q, 1, 0, 0, None)
                rcopy(view, view, self.zsend.at[q], self.zrecv.at[q], self.z_partner()).wait_recv()
            for to in ((1, 0), (-1, 0), (0, 1), (0, -1)):
                self.send(q, zsel, 0, 0, None, to, src)
        elif n in (1, 2):
            d = -1 if n == 1 else 1
            self.recv(q, zsel, d, 0)
            self.send(q, zsel, d, 0, 0 if n == 1 else 1, (-d, 0))
            for to in ((0, 1), (0, -1)):
                self.send(q, zsel, d, 0, None, to)
        elif n == 4:
            self.recv(q, zsel, 2, 0, 0)
            self.recv(q, zsel, 2, 0, 1)
            for to in ((0, 1), (0, -1)):
                self.send(q, zsel, 2, 0, None, to)
        elif n in (3, 5, 6, 7):
            da = {3: 0, 5: -1, 6: 1, 7: 2}[n]
            for d, half in ((-1, 0), (1, 1)):
                self.recv(q, zsel, da, d)
                self.send(q, zsel, da, d, half, (0, -d))
        else:
            for da in (0, -1, 1, 2):
                for half in (0, 1):
                    self.recv(q, zsel, da, 2, half)

    def drain(self):
        for copy in self.sent:
            copy.wait_send()


ORDER = [(0, 0), (0, 1), (0, 2), (0, 3), (1, 0), (0, 4), (0, 5), (0, 6), (1, 1), (1, 2), (0, 7), (1, 3), (1, 4), (1, 5), (1, 6), (1, 7)]
GATHER_SENDS = 80


def gather_sems():
    dma = pltpu.SemaphoreType.DMA
    return [dma((2,)), dma((2,)), dma((GATHER_SENDS,)), dma((2, 2, SIDE * SIDE, 2)), dma((2,))]


def greet(peers):
    barrier = pltpu.get_barrier_semaphore()
    for peer in peers:
        pl.semaphore_signal(barrier, inc=1, device_id=peer, device_id_type=MESH)
    pl.semaphore_wait(barrier, len(peers))


def conv_kernel(
    w_ref, prep_ref, edge_ref, skip_ref, chan_ref, enc_ref,
    F, X, P2, S2, H, acc, stage, zs, zr, ss, rs, ls, xs, xr,
):
    dp, seq, mp = (lax.axis_index(a) for a in ("dp", "seq", "mp"))
    core = dp % CORES
    other = dp - core + (1 - core)
    rows, cut = w_ref.shape[0], 112
    taps, depth = 5, rows // 5
    width = F.shape[4]

    def cols(n, count=1):
        return pl.ds(pl.multiple_of(n * width, width), count * width)

    g = Gather(F, lambda q: w_ref.at[:, cols(CORES * core + q)], rows, cut, zs, zr, ss, rs, ls, mirror=True)
    place = seq * 2 + mp
    last_place = SIDE * SIDE * 2 - 1
    after, before = (place + 1) % (last_place + 1), (place + last_place) % (last_place + 1)

    def at(p, d):
        return {"dp": d, "seq": p // 2, "mp": p % 2}

    partner = {"dp": other}
    greet(g.peers() + [partner, at(after, dp), at(after, other), at(before, dp), at(before, other)])

    g.start_z()
    extra = []
    n = 0
    for w, d in ((0, dp), (1, other)):
        extra.append(rcopy(edge_ref.at[1], H.at[w, 0], xs.at[n], xr.at[n], at(after, d)))
        extra.append(rcopy(edge_ref.at[0], H.at[w, 1], xs.at[n + 1], xr.at[n + 1], at(before, d)))
        n += 2
    extra.append(rcopy(prep_ref, P2, xs.at[4], xr.at[4], partner))
    extra.append(rcopy(skip_ref.at[:, cols(CORES * (1 - core), 2)], S2, xs.at[5], xr.at[5], partner))
    for copy in extra:
        copy.start()
    for q in (0, 1):
        g.stage(q, 0, 0)

    def spread(w, n):
        zabs, lanes = n // 3, pl.ds((n % 3) * 256, 256)
        chan = chan_ref[:, n * 256 : (n + 1) * 256]
        cin = prep_ref.shape[2]
        pick = (lax.broadcasted_iota(jnp.int32, (cin, 256), 0) == chan).astype(jnp.float32).astype(jnp.bfloat16)
        src = prep_ref if w == 0 else P2
        height = src.shape[1]
        dot = functools.partial(jnp.dot, preferred_element_type=jnp.float32)
        even, odd = dot(src[0], pick), dot(src[1], pick)
        prev, nxt = dot(H[w, 0], pick), dot(H[w, 1], pick)
        prev = jnp.where(place == 0, 0.0, prev)
        nxt = jnp.where(place == last_place, 0.0, nxt)
        row = lax.broadcasted_iota(jnp.int32, (height, 256), 0)
        for m, (arr, halo, shift) in enumerate((
            (even, prev[14:15], 1), (odd, prev[15:16], 1), (even, None, 0), (odd, None, 0),
            (even, nxt[0:1], -1), (odd, nxt[1:2], -1),
        )):
            if shift == 1:
                arr = jnp.where(row == 0, halo, pltpu.roll(arr, 1, 0))
            elif shift == -1:
                arr = jnp.where(row == height - 1, halo, pltpu.roll(arr, height - 1, 0))
            X[w, zabs, m, :, lanes] = arr.astype(jnp.bfloat16)

    def do_spread(k):
        w, n = divmod(k, 6)
        if k == 0:
            for copy in extra:
                copy.wait_recv()
        spread(w, n)

    todo = list(range(12))
    for i, (zsel, st) in enumerate(ORDER[1:]):
        if i >= 1 and todo:
            do_spread(todo.pop(0))
        for q in (0, 1):
            g.stage(q, zsel, st)
    while todo:
        do_spread(todo.pop(0))

    for local in g.pending_local:
        local.wait()

    def conv(zsel, colours):
        za = g.z_of(zsel)
        for q in colours:
            def tap(k, carry):
                lhs = X[:, za, pl.ds(k, 2)].reshape(acc.shape[1], -1)
                rhs = F[q, za, :, pl.ds(pl.multiple_of(k * depth, 16), depth), :].reshape(-1, width)
                acc[q] += jnp.dot(lhs, rhs, preferred_element_type=jnp.float32)
                return carry
            lax.fori_loop(0, taps, tap, 0)

    acc[...] = jnp.zeros_like(acc)
    for q in (0, 1):
        g.stage(q, 0, 8)
    conv(0, (0, 1))
    for q in (0, 1):
        g.stage(q, 1, 8)
    half = acc.shape[1] // 2
    coarse = half // 2
    finals = []
    for q in (0, 1):
        conv(1, (q,))
        total = acc[q, half:] + S2[:, q * width : (q + 1) * width].astype(jnp.float32)
        stage[q] = jnp.maximum(total[:coarse], total[coarse:]).astype(jnp.bfloat16)
        copy = rcopy(stage.at[q], enc_ref.at[:, cols(CORES * core + q)], xs.at[6 + q], xr.at[6 + q], partner)
        copy.start()
        finals.append(copy)
    for q in (0, 1):
        total = acc[q, :half] + skip_ref[:, cols(CORES * core + q)].astype(jnp.float32)
        enc_ref[:, cols(CORES * core + q)] = jnp.maximum(total[:coarse], total[coarse:]).astype(jnp.bfloat16)
    for q in (0, 1):
        view = enc_ref.at[:, cols(CORES * (1 - core) + q)]
        rcopy(stage.at[q], view, xs.at[6 + q], xr.at[6 + q], partner).wait_recv()
    g.drain()
    for copy in extra + finals:
        copy.wait_send()


def encode(filt, prep, edge, skip, chan):
    vm = pl.BlockSpec(memory_space=pltpu.VMEM)
    dma = pltpu.SemaphoreType.DMA
    rows, model_dim = filt.shape
    width = model_dim // 4
    coarse = prep.shape[1]
    kdepth = SIDE * SIDE * rows // 5
    return pl.pallas_call(
        conv_kernel,
        out_shape=jax.ShapeDtypeStruct((coarse, model_dim), jnp.bfloat16),
        in_specs=[vm] * 5,
        out_specs=vm,
        scratch_shapes=[
            pltpu.VMEM((2, 2, SIDE * SIDE, rows, width), jnp.bfloat16),
            pltpu.VMEM((2, 2, 6, coarse, kdepth), jnp.bfloat16),
            pltpu.VMEM(prep.shape, jnp.bfloat16),
            pltpu.VMEM((2 * coarse, 2 * width), jnp.bfloat16),
            pltpu.VMEM((2, 2, 16, prep.shape[2]), jnp.bfloat16),
            pltpu.VMEM((2, 4 * coarse, width), jnp.float32),
            pltpu.VMEM((2, coarse, width), jnp.bfloat16),
        ] + gather_sems() + [dma((8,)), dma((8,))],
        compiler_params=pltpu.CompilerParams(collective_id=0, has_side_effects=True, vmem_limit_bytes=60 << 20),
        name="encode",
    )(filt, prep, edge, skip, chan)


def share_kernel(src_ref, pair_ref, out_ref, turn_ref, zs, zr, ss, rs, ls, ts, tr):
    rows = src_ref.shape[1]
    g = Gather(out_ref, lambda q: src_ref.at[q], rows, rows // 2, zs, zr, ss, rs, ls)
    n = pair_ref.shape[0]
    place = g.seq * 2 + g.mp
    others = [(place + d) % n for d in range(1, n)]
    devices = [{"seq": p // 2, "mp": p % 2} for p in others]
    greet(devices)
    g.start_z()
    turns = [rcopy(pair_ref.at[p], turn_ref.at[place], ts.at[d], tr.at[place], devices[d]) for d, p in enumerate(others)]
    waiting = list(turns)
    turn_ref[place] = pair_ref[place]
    for zsel, st in ORDER + [(0, 8), (1, 8)]:
        for q in (0, 1):
            g.stage(q, zsel, st)
        for copy in waiting[:2]:
            copy.start()
        waiting = waiting[2:]
    for d, p in enumerate(others):
        view = turn_ref.at[p]
        rcopy(view, view, ts.at[d], tr.at[p], devices[d]).wait_recv()
    for local in g.pending_local:
        local.wait()
    g.drain()
    for copy in turns:
        copy.wait_send()


def share(src, pair):
    vm = pl.BlockSpec(memory_space=pltpu.VMEM)
    dma = pltpu.SemaphoreType.DMA
    return pl.pallas_call(
        share_kernel,
        out_shape=(
            jax.ShapeDtypeStruct((2, 2, SIDE * SIDE) + src.shape[1:], src.dtype),
            jax.ShapeDtypeStruct(pair.shape, pair.dtype),
        ),
        in_specs=[vm, vm],
        out_specs=(vm, vm),
        scratch_shapes=gather_sems() + [dma((pair.shape[0],))] * 2,
        compiler_params=pltpu.CompilerParams(collective_id=1, has_side_effects=True, vmem_limit_bytes=32 << 20),
        name="share",
    )(src, pair)


def attend_kernel(g_ref, q_ref, kv_ref, out_ref, mix_ref, R1, R2, fin, s1, r1, s2, r2, s3, r3, key_dim, value_dim):
    dp, seq, mp = (lax.axis_index(a) for a in ("dp", "seq", "mp"))

    def attend(first, end):
        def two(p, carry):
            mixes = []
            for e in (0, 1):
                query = q_ref[:, pl.ds(pl.multiple_of((2 * p + e) * key_dim, key_dim), key_dim)]
                mixed, norm = 0.0, 0.0
                for c in range(4):
                    keys = kv_ref[c // 2, c % 2, :, :, :key_dim].reshape(-1, key_dim)
                    values = kv_ref[c // 2, c % 2, :, :, key_dim : key_dim + value_dim].reshape(-1, value_dim)
                    score = lax.dot_general(query, keys, (((1,), (1,)), ((), ())), preferred_element_type=jnp.float32)
                    weight = jnp.exp(logit_cap * jnp.tanh(score * (1.0 / logit_cap)))
                    norm += jnp.sum(weight, axis=-1, keepdims=True)
                    mixed += jnp.dot(weight.astype(jnp.bfloat16), values, preferred_element_type=jnp.float32)
                mixes.append(mixed / norm)
            both = jnp.concatenate(mixes, axis=1).astype(jnp.bfloat16)
            mix_ref[:, pl.ds(pl.multiple_of(p * 2 * value_dim, 2 * value_dim), 2 * value_dim)] = both
            return carry
        lax.fori_loop(first, end, two, 0)

    n1, n2 = SIDE * SIDE, Z_LO * CORES * 2
    rows = g_ref.shape[0] // n1
    plane = [{"seq": (seq + d) % n1} for d in range(1, n1)]
    mine = dp * 2 + mp
    column = []
    for d in range(1, n2):
        t = (mine + d) % n2
        column.append({"dp": t // 2, "mp": t % 2})
    greet(plane + column)
    sent = []
    for d, dev in enumerate(plane):
        c = rcopy(g_ref.at[pl.ds(pl.multiple_of(dev["seq"] * rows, rows), rows)], R1.at[seq], s1.at[d], r1.at[seq], dev)
        c.start()
        sent.append(c)
    own = g_ref[pl.ds(pl.multiple_of(seq * rows, rows), rows)]
    R1[seq] = own
    attend(0, 1)
    for d, dev in enumerate(plane):
        view = R1.at[dev["seq"]]
        rcopy(view, view, s1.at[d], r1.at[dev["seq"]], dev).wait_recv()
    fin[0] = jnp.sum(R1[...], axis=0)
    for d, dev in enumerate(column):
        c = rcopy(fin.at[0], R2.at[mine], s2.at[d], r2.at[mine], dev)
        c.start()
        sent.append(c)
    R2[mine] = fin[0]
    attend(1, 2)
    for d, dev in enumerate(column):
        t = dev["dp"] * 2 + dev["mp"]
        rcopy(R2.at[t], R2.at[t], s2.at[d], r2.at[t], dev).wait_recv()
    fin[1] = jnp.sum(R2[...], axis=0)
    piece = pl.ds(pl.multiple_of(seq * rows, rows), rows)
    for d, dev in enumerate(plane):
        c = rcopy(fin.at[1], out_ref.at[piece], s3.at[d], r3.at[seq], dev)
        c.start()
        sent.append(c)
    out_ref[piece] = fin[1]
    attend(2, q_ref.shape[1] // key_dim // 2)
    for d, dev in enumerate(plane):
        view = out_ref.at[pl.ds(pl.multiple_of(dev["seq"] * rows, rows), rows)]
        rcopy(view, view, s3.at[d], r3.at[dev["seq"]], dev).wait_recv()
    for c in sent:
        c.wait_send()


def attend_and_total(term, queries, shared, key_dim, value_dim):
    vm = pl.BlockSpec(memory_space=pltpu.VMEM)
    dma = pltpu.SemaphoreType.DMA
    rows = term.shape[0] // (SIDE * SIDE)
    n = SIDE * SIDE
    block = (n, rows, term.shape[1])
    mixed = (queries.shape[0], queries.shape[1] // key_dim * value_dim)
    return pl.pallas_call(
        functools.partial(attend_kernel, key_dim=key_dim, value_dim=value_dim),
        out_shape=(jax.ShapeDtypeStruct(term.shape, term.dtype), jax.ShapeDtypeStruct(mixed, jnp.bfloat16)),
        in_specs=[vm] * 3,
        out_specs=(vm, vm),
        scratch_shapes=[pltpu.VMEM(block, jnp.float32), pltpu.VMEM(block, jnp.float32), pltpu.VMEM((2,) + block[1:], jnp.float32)]
        + [dma((n,))] * 6,
        compiler_params=pltpu.CompilerParams(collective_id=2, has_side_effects=True, vmem_limit_bytes=40 << 20),
        name="attend",
    )(term, queries, shared)


def per_device(
    features, conv_weight, norm_gain, query_weight, keyval_weight, head_scale, output_weight, pair_weight,
    pair_input, flip_weight, pair_cotangent,
):
    fine_rows, in_channels = features.shape[1:]
    coarse = fine_rows // 2
    model_dim = output_weight.shape[1]
    key_dim = query_weight.shape[1] // head_scale.shape[0]
    value_dim = keyval_weight.shape[1] - key_dim
    pair_dim = flip_weight.shape[0]
    taps, per_shard = conv_weight.shape[:2]
    padded = 48

    filt = jnp.pad(conv_weight, ((0, 0), (0, padded - per_shard), (0, 0))).reshape(taps * padded, model_dim)
    prepared = prepare(features[0])
    edge = jnp.stack([prepared[:16], prepared[fine_rows - 16 :]])
    wanted = np.arange(fine_rows).reshape(coarse, 2).T.reshape(-1)
    split = (jnp.asarray(wanted.astype(np.int32))[:, None] == lax.broadcasted_iota(jnp.int32, (1, fine_rows), 1)).astype(jnp.bfloat16)
    prep = jnp.dot(split, prepared, preferred_element_type=jnp.float32).astype(jnp.bfloat16)
    prep = prep.reshape(2, coarse, in_channels)
    skip = jnp.dot(split, features[0], preferred_element_type=jnp.float32).astype(jnp.bfloat16)
    skip = jnp.pad(skip, ((0, 0), (0, model_dim - in_channels)))
    lane = np.arange(2 * SIDE * SIDE * padded)
    zh, sq, ch = lane // (SIDE * SIDE * padded), (lane // padded) % (SIDE * SIDE), lane % padded
    chan = np.where(ch < per_shard, per_shard * (2 * sq + zh) + ch, -1).astype(np.int32)[None]
    encoded = encode(filt, prep, edge, skip, jnp.asarray(chan))

    widened = encoded.astype(jnp.float32)
    normed = (root_norm(widened) * norm_gain).astype(jnp.bfloat16)
    keyvals = jnp.dot(normed, keyval_weight, preferred_element_type=jnp.float32).astype(jnp.bfloat16)
    pooled = jnp.mean(widened.reshape(coarse // PAIR_POOL, PAIR_POOL, model_dim), axis=1).astype(jnp.bfloat16)
    feats = jnp.dot(pooled, pair_weight, preferred_element_type=jnp.float32).astype(jnp.bfloat16)
    pair_rows = feats.shape[0]
    spare = jnp.pad(feats.reshape(-1, 64), ((0, coarse - feats.size // 64), (0, 0)))
    block = jnp.concatenate([keyvals, spare], axis=1).reshape(2, coarse // 2, -1)
    blocks = 2 * SIDE * SIDE
    pieces = pair_input[0].reshape(pair_rows, blocks, -1, pair_dim).transpose(1, 0, 2, 3)
    shared, turned_in = share(block, pieces.reshape(blocks, -1, pair_dim))
    turned_in = turned_in.reshape(blocks * pair_rows, -1, pair_dim)
    scale_row = jnp.repeat(head_scale, key_dim) / math.sqrt(key_dim)
    queries = (jnp.dot(normed, query_weight, preferred_element_type=jnp.float32) * scale_row).astype(jnp.bfloat16)

    feats_all = shared[0, :, :, : feats.size // 64, key_dim + value_dim :]
    feats_all = feats_all.transpose(1, 0, 2, 3).reshape(-1, 2 * pair_dim).astype(jnp.float32)
    pair_q, pair_k = feats[:, :pair_dim].astype(jnp.float32), feats[:, pair_dim:].astype(jnp.float32)
    q_all, k_all = feats_all[:, :pair_dim], feats_all[:, pair_dim:]
    summed = (pair_input[0].astype(jnp.float32) + pair_q[:, None, :] * k_all[None]).astype(jnp.bfloat16)
    flipped = (turned_in.astype(jnp.float32) + q_all[:, None, :] * pair_k[None]).astype(jnp.bfloat16)
    turned = jnp.einsum("bac,cd->abd", flipped, flip_weight, preferred_element_type=jnp.float32)
    pair_out = (summed.astype(jnp.float32) + turned).astype(jnp.bfloat16)
    grad_term = jnp.einsum("bac,abd->cd", flipped, pair_cotangent[0], preferred_element_type=jnp.float32)
    grad_flip, heads_out = attend_and_total(grad_term, queries, shared, key_dim, value_dim)

    block_out = (widened + jnp.dot(heads_out, output_weight, preferred_element_type=jnp.float32)).astype(jnp.bfloat16)
    return (block_out[None], pair_out[None], grad_flip)


def solution(mesh):
    rows = P("dp", ("seq", "mp"), None)
    pair = P("dp", ("seq", "mp"), None, None)
    placed = (rows, P(None, ("seq", "mp"), None), P(), P(), P(), P(), P(), P(), pair, P(), pair)
    return jax.shard_map(per_device, mesh=mesh, in_specs=placed, out_specs=(rows, pair, P()), check_vma=False)
```
